512 devices in a mesh: gx: 8 (over x, core), gy: 8 (over y), obs: 8 (over z).
Axes of the slice: x: 4, y: 8, z: 8, core: 2. Of those that a mesh axis runs over, the one named last changes fastest.
Arguments:
- control: float32 [4, 8, 1024, 1024], P(None, 'obs', 'gy', 'gx'), may hold values from -6 to 6
- diffusivity: float32 [2, 8, 1024, 1024], P(None, 'obs', 'gy', 'gx'), may hold values from 0.12 to 0.245
- prof_tile: int32 [32768, 1], P(('gx', 'gy')), may hold values from 0 to 63; in each aligned block of 512 rows (0 to 511, 512 to 1023, ...) at most 16 rows name the same one
- prof_cell: int32 [32768], P(('gx', 'gy')), may hold values from 0 to 16383
- obs_prof: int32 [262144], P(('gx', 'gy', 'obs')), may hold values from 0 to 511
- obs_field: int32 [262144], P(('gx', 'gy', 'obs')), may hold values from 0 to 3
- obs_level: int32 [262144], P(('gx', 'gy', 'obs')), may hold values from 0 to 6
- obs_weight: float32 [262144], P(('gx', 'gy', 'obs')), may hold values from 0 to 1
- innovation: float32 [262144], P(('gx', 'gy', 'obs')), may hold values from -6 to 6
- obs_precision: float32 [262144], P(('gx', 'gy', 'obs')), may hold values from 0.25 to 4
Outputs:
- gradient: float32 [4, 8, 1024, 1024], P(None, 'obs', 'gy', 'gx')
- departures: float32 [262144], P(('gx', 'gy', 'obs'))
The draws below stay inside these ranges and needn't reach their ends.
Inputs may be any that keep to these rules, and one draw needn't show every extreme that they name: `prof_tile`: in each aligned block of 512 rows (the profiles of one tile) no tile is named by more than 16 rows; in some blocks one tile is named by exactly 16 rows.
All inputs are finite; a program needn't handle non-finite values.
Results may differ from the reference program's by a relative error of at most 0.00002.
Values sent between devices are 32-bit elements; how exact they have to be, the bound alone decides.
No kernel may reach another device: no remote copies, remote signals or barrier semaphores. Data moves between devices by JAX's collectives and lax.ppermute only.
A program may use at most 64 MiB of HBM per device.

```python
import math
import jax
import jax.numpy as jnp
import numpy as np
from jax import lax

F = 4
CY = 128
CX = 128
PROF_DEV = 512
OBS_DEV = 512
STEPS = 10
LEV = 8
NY = 1024
NX = 1024
PROFILES = 32768
OBSERVATIONS = 262144
CAP = 16
N_GX = 8
N_GY = 8
N_OBS = 8


def place_ends(result, stream_key, smallest, top_value):
    longest = result.shape.index(max(result.shape))
    spots = []
    for shift in (0, 1):
        where = [jax.random.randint(jax.random.fold_in(stream_key, axis), (), 0, length) for axis, length in enumerate(result.shape)]
        where[longest] = (where[longest] + shift) % result.shape[longest]
        spots.append(tuple(where))
    return result.at[spots[0]].set(smallest).at[spots[1]].set(top_value)


def block_levels(key, shape, pieces, smallest, largest):
    loudness, own = 1.0, jax.random.fold_in(key, 6)
    for dim, blocks in pieces:
        draws = jnp.exp(jax.random.uniform(jax.random.fold_in(own, dim), (blocks,), jnp.float32, smallest / len(pieces), largest / len(pieces)))
        loudness = loudness * jnp.repeat(draws, shape[dim] // blocks).reshape([-1 if axis == dim else 1 for axis in range(len(shape))])
    return loudness


def routed_block(stream_key, own, number, rows, count, top, bound, slope):
    sequence = jax.random.permutation(stream_key, count)
    crowded, usual = portions_of(count, rows * top, bound, slope, True), portions_of(count, rows * top, bound, slope, False)
    places = jnp.arange(count)

    def named(lengths, offset_by):
        used = int((lengths > 0).sum())
        fixed = max(1, used // 4)
        moved = fixed + (places - fixed + offset_by * (used - fixed)) % max(1, count - fixed)
        return jnp.zeros((count,), jnp.int32).at[sequence[jnp.where(places < fixed, places, moved)]].set(jnp.asarray(lengths, jnp.int32))

    lengths = jnp.where(number % 4 == 0, named(crowded, number // 4), named(usual, number - number // 4 - 1))
    mixed = jax.random.permutation(jax.random.fold_in(own, 3), count)
    donor, receiver = mixed[0:count // 2 * 2:2], mixed[1:count // 2 * 2:2]
    slack = jnp.minimum(lengths[donor] - 1, bound - lengths[receiver]) // 2
    slack = jnp.where((donor == sequence[0]) | (receiver == sequence[0]) | (lengths[receiver] == 0), 0, jnp.maximum(slack, 0))
    moved = jax.random.randint(jax.random.fold_in(own, 4), (count // 2,), 0, 1 << 20) % (slack + 1)
    lengths = lengths.at[donor].add(-moved).at[receiver].add(moved)
    items = jnp.searchsorted(jnp.cumsum(lengths), jnp.arange(rows * top), side="right").astype(jnp.int32)
    listing = items.reshape(top, rows).T
    listing = listing[jax.random.permutation(jax.random.fold_in(own, 1), rows)]
    offset_by = jax.random.randint(jax.random.fold_in(own, 2), (rows, 1), 0, top)
    return jnp.take_along_axis(listing, (jnp.arange(top)[None, :] + offset_by) % top, axis=1)


def portions_of(amount, total, reach, skew, full):
    loads = [(1 << 20) // math.isqrt(grade ** skew) + 1 for grade in range(1, amount + 1)]
    largest = reach if full else min(reach, max(-(-total // amount), total * loads[0] // sum(loads)))
    least = 1 if total - largest >= amount - 1 else 0
    counts, spare = [largest] + [least] * (amount - 1), total - largest - least * (amount - 1)
    while spare > 0:
        candidates = [i for i in range(1, amount) if counts[i] < largest] or [i for i in range(1, amount) if counts[i] < reach]
        mass, budget = sum([loads[i] for i in candidates]), spare
        for i in candidates:
            more = min(reach - counts[i], max(1, budget * loads[i] // mass), spare)
            counts[i] = counts[i] + more
            spare = spare - more
    return np.array(counts)


def noise(rng, shape, deviation, reach, cuts=(), held_as=jnp.bfloat16):
    factor_of = block_levels(rng, shape, cuts, -0.22, 0.18) if cuts else 1.0
    values = jax.random.normal(rng, shape, jnp.float32) * deviation * factor_of
    return jnp.minimum(jnp.maximum(values, -reach), reach).astype(held_as)


def setup_inputs(seed: int = 0) -> dict:
    keys = jax.random.split(jax.random.key(seed), 11)
    control = noise(keys[0], (F, LEV, NY, NX), 1.0, 6.0, ((1, 8), (2, 8), (3, 8)), jnp.float32)
    diffusivity = jnp.clip(jnp.exp(math.log(0.245) - 0.7137665 * jax.random.uniform(keys[1], (2, LEV, NY, NX), jnp.float32) ** block_levels(keys[1], (2, LEV, NY, NX), ((1, 8), (2, 8), (3, 8)), -0.2, 0.2)), 0.12, 0.245)
    prof_tile_keys = jax.random.split(jax.random.fold_in(keys[2], 1), PROFILES // PROF_DEV)
    prof_tile_turns = jax.random.permutation(jax.random.fold_in(keys[2], 3), PROFILES // PROF_DEV)
    prof_tile = jax.vmap(lambda own, number: routed_block(jax.random.fold_in(keys[2], 2), own, number, PROF_DEV, N_GX * N_GY, 1, CAP, 2))(prof_tile_keys, prof_tile_turns).reshape((PROFILES, 1))
    prof_cell = place_ends(jax.random.randint(keys[3], (PROFILES,), 0, CY * CX), jax.random.fold_in(keys[3], 1), 0, (CY * CX) - 1).astype(jnp.int32)
    obs_prof = place_ends(jax.random.randint(keys[4], (OBSERVATIONS,), 0, PROF_DEV), jax.random.fold_in(keys[4], 1), 0, PROF_DEV - 1).astype(jnp.int32)
    obs_field = place_ends(jax.random.randint(keys[5], (OBSERVATIONS,), 0, F), jax.random.fold_in(keys[5], 1), 0, F - 1).astype(jnp.int32)
    obs_level = place_ends(jax.random.randint(keys[6], (OBSERVATIONS,), 0, LEV - 1), jax.random.fold_in(keys[6], 1), 0, (LEV - 1) - 1).astype(jnp.int32)
    obs_weight = jnp.clip(1.0 * jax.random.uniform(keys[7], (OBSERVATIONS,), jnp.float32) ** block_levels(keys[7], (OBSERVATIONS,), ((0, 512),), -0.2, 0.2), 0.0, 1.0)
    innovation = noise(keys[8], (OBSERVATIONS,), 1.0, 6.0, ((0, 512),), jnp.float32)
    obs_precision = jnp.clip(jnp.exp(math.log(4.0) - 2.7725887 * jax.random.uniform(keys[9], (OBSERVATIONS,), jnp.float32) ** block_levels(keys[9], (OBSERVATIONS,), ((0, 512),), -0.2, 0.2)), 0.25, 4.0)
    return dict(control=control, diffusivity=diffusivity, prof_tile=prof_tile, prof_cell=prof_cell, obs_prof=obs_prof, obs_field=obs_field, obs_level=obs_level, obs_weight=obs_weight, innovation=innovation, obs_precision=obs_precision)


def advance(values, east_rate, north_rate):
    east_flux = east_rate * (jnp.roll(values, -1, 2) - values)
    west_flux = jnp.roll(east_rate, 1, 2) * (jnp.roll(values, 1, 2) - values)
    north_flux = north_rate * (jnp.roll(values, -1, 1) - values)
    south_flux = jnp.roll(north_rate, 1, 1) * (jnp.roll(values, 1, 1) - values)
    return values + east_flux + west_flux + north_flux + south_flux


def diffuse(field, east_rate, north_rate):
    def smooth(field_plane):
        def sweep(step_index, values):
            return advance(values, east_rate, north_rate)
        return lax.fori_loop(0, STEPS, sweep, field_plane)
    return lax.map(smooth, field)


def reference(control, diffusivity, prof_tile, prof_cell, obs_prof, obs_field, obs_level, obs_weight, innovation, obs_precision):
    row_index = jnp.arange(NY)
    east_rate = diffusivity[0]
    north_rate = diffusivity[1] * (row_index != NY - 1).astype(jnp.float32)[None, :, None]
    increment = diffuse(control, east_rate, north_rate)
    holder_of = prof_tile[:, 0]
    lat_index = (holder_of % N_GY) * CY + prof_cell // CX
    lon_index = (holder_of // N_GY) * CX + prof_cell % CX
    columns = increment[:, :, lat_index, lon_index]
    owner_tile = jnp.arange(OBSERVATIONS, dtype=jnp.int32) // (OBS_DEV * N_OBS)
    profile = owner_tile * PROF_DEV + obs_prof
    flat_columns = columns.reshape(-1)
    lower_index = (obs_field * LEV + obs_level) * PROFILES + profile
    upper_index = lower_index + PROFILES
    observed = obs_weight * flat_columns[lower_index] + (1.0 - obs_weight) * flat_columns[upper_index]
    departures = obs_precision * (observed - innovation)
    adjoint = jnp.zeros((F * LEV * PROFILES,), jnp.float32)
    adjoint = adjoint.at[lower_index].add(obs_weight * departures)
    adjoint = adjoint.at[upper_index].add((1.0 - obs_weight) * departures)
    adjoint = adjoint.reshape(F, LEV, PROFILES)
    pulled = jnp.zeros(control.shape, jnp.float32).at[:, :, lat_index, lon_index].add(adjoint)
    gradient = control + diffuse(pulled, east_rate, north_rate)
    return gradient, departures
```

```python
import jax
import jax.numpy as jnp
from jax import lax
from jax.experimental import pallas as pl
from jax.experimental.pallas import tpu as pltpu
from jax.sharding import PartitionSpec as P

STEPS = 10
HALO = STEPS
ROWS = 16
PITCH = 2 * HALO
PAD = 8
F32, BF16, I32 = jnp.float32, jnp.bfloat16, jnp.int32


def lanes(shape):
    return lax.broadcasted_iota(I32, shape, len(shape) - 1)


def subs(shape):
    return lax.broadcasted_iota(I32, shape, len(shape) - 2)


def split3(x):
    hi = x.astype(BF16)
    rest = x - hi.astype(F32)
    mid = rest.astype(BF16)
    low = (rest - mid.astype(F32)).astype(BF16)
    return hi, mid, low


def one_hot(flags):
    return jnp.where(flags, 1.0, 0.0).astype(BF16)


def dot_nn(a, b):
    return lax.dot_general(a, b, (((1,), (0,)), ((), ())), preferred_element_type=F32)


def dot_nt(a, b):
    return lax.dot_general(a, b, (((1,), (1,)), ((), ())), preferred_element_type=F32)


def call(body, outs, args, scratch=(), flops=1_000_000, smem=()):
    vmem = pl.BlockSpec(memory_space=pltpu.VMEM)
    moved = sum(a.size * 4 for a in args) + sum(4 * _size(s) for s in outs)
    return pl.pallas_call(
        body,
        out_shape=[jax.ShapeDtypeStruct(s, F32) for s in outs],
        in_specs=[vmem] * len(args),
        out_specs=[vmem] * len(outs),
        scratch_shapes=list(scratch),
        cost_estimate=pl.CostEstimate(flops=flops, bytes_accessed=moved, transcendentals=0),
        name=body.__name__,
    )(*args)


def _size(shape):
    n = 1
    for s in shape:
        n *= s
    return n


def masked_north(rate_ref):
    north = rate_ref[1]
    top = lax.axis_index("gy") == lax.axis_size("gy") - 1
    return jnp.where(top & (subs(north.shape) == north.shape[0] - 1), 0.0, north)


def pack_edges(arrays, east_ref, west_ref):
    lane = lanes(arrays[0].shape)
    east = jnp.zeros(arrays[0].shape, F32)
    west = jnp.zeros(arrays[0].shape, F32)
    for a, x in enumerate(arrays):
        width = x.shape[-1]
        low = a * PITCH + HALO
        moved = pltpu.roll(x, (low - (width - HALO)) % width, 1)
        east = jnp.where((lane >= low) & (lane < low + HALO), moved, east)
        low = a * PITCH
        moved = pltpu.roll(x, low % width, 1) if low else x
        west = jnp.where((lane >= low) & (lane < low + HALO), moved, west)
    east_ref[...] = east
    west_ref[...] = west


def pack_inputs(ctl, rate, prof, field, level, weight, innov, prec, east, west, obs):
    pack_edges([ctl[f] for f in range(ctl.shape[0])] + [rate[0], masked_north(rate)], east, west)
    index = ((field[...] * 8 + level[...]) * 512 + prof[...]).astype(F32)
    rows = jnp.concatenate([index, weight[...], innov[...], prec[...]], axis=0)
    for z in range(obs.shape[0] // rows.shape[0]):
        obs[pl.ds(z * rows.shape[0], rows.shape[0]), :] = rows


def north_south(arrays, strip, north_ref, south_ref):
    for a, x in enumerate(arrays + [strip]):
        north_ref[a] = x[x.shape[0] - ROWS :]
        south_ref[a] = x[:ROWS]


def edges_first(ctl, rate, left, right, strip, north, south):
    joined = left[...] + right[...]
    strip[...] = joined
    arrays = [ctl[f] for f in range(ctl.shape[0])] + [rate[0], masked_north(rate)]
    north_south(arrays, joined, north, south)


def edges_second(pulled, left, right, strip, north, south):
    joined = left[...] + right[...]
    strip[...] = joined
    north_south([pulled[f] for f in range(pulled.shape[0])], joined, north, south)


def unpack(block, a):
    width = block.shape[-1]
    east = pltpu.roll(block, (-a * PITCH) % width, 1) if a else block
    west = pltpu.roll(block, (width - HALO - a * PITCH - HALO) % width, 1)
    return jnp.where(lanes(block.shape) < width // 2, east, west)


def blocks(own, south, north):
    height = own.shape[0]
    return ((PAD, south), (PAD + ROWS, own), (PAD + ROWS + height, north))


def turned(main, beyond, by):
    width = main.shape[-1]
    edge = lanes(main.shape) == (0 if by == 1 else width - 1)
    a = pltpu.roll(main, by % width, 1)
    b = pltpu.roll(beyond, by % width, 1)
    return jnp.where(edge, b, a), jnp.where(edge, a, b)


def one_step(source, coef, store, first, last):
    fields = source.shape[0] // 2
    for tile in range(first, last):
        row = PAD + 8 * tile
        here, up, down = pl.ds(row, 8), pl.ds(row + 1, 8), pl.ds(row - 1, 8)
        c = [coef[i, pl.ds(8 * tile, 8), :] for i in range(10)]
        for f in range(fields):
            m, s = source[2 * f, here, :], source[2 * f + 1, here, :]
            me, se = turned(m, s, -1)
            mw, sw = turned(m, s, 1)
            new_m = c[0] * m + c[2] * me + c[4] * mw + c[6] * source[2 * f, up, :]
            new_m = new_m + c[8] * source[2 * f, down, :]
            new_s = c[1] * s + c[3] * se + c[5] * sw + c[7] * source[2 * f + 1, up, :]
            new_s = new_s + c[9] * source[2 * f + 1, down, :]
            store(f, tile, new_m, new_s)


def ten_steps(a, b, coef, finish, tiles):
    def into(target):
        def store(f, tile, main, beyond):
            target[2 * f, pl.ds(PAD + 8 * tile, 8), :] = main
            target[2 * f + 1, pl.ds(PAD + 8 * tile, 8), :] = beyond

        return store

    one_step(a, coef, into(b), 0, tiles)

    def body(_, carry):
        one_step(b, coef, into(a), 1, tiles - 1)
        one_step(a, coef, into(b), 1, tiles - 1)
        return carry

    lax.fori_loop(0, STEPS // 2 - 1, body, 0)

    def store(f, tile, main, beyond):
        finish(f, 8 * tile - ROWS, main)

    one_step(b, coef, store, ROWS // 8, tiles - ROWS // 8)


def load_field(a, own, strip, south, north):
    fields = own.shape[0]
    for f in range(fields):
        for row, block in blocks(own[f], south[f], north[f]):
            a[2 * f, pl.ds(row, block.shape[0]), :] = block
    for row, block in blocks(strip[...], south[south.shape[0] - 1], north[north.shape[0] - 1]):
        for f in range(fields):
            a[2 * f + 1, pl.ds(row, block.shape[0]), :] = unpack(block, f)
    clear = jnp.zeros((PAD, a.shape[2]), F32)
    for plane in range(a.shape[0]):
        a[plane, pl.ds(0, PAD), :] = clear
        a[plane, pl.ds(a.shape[1] - PAD, PAD), :] = clear


def diffuse_control(ctl, rate, strip, south, north, inc, coef, a, b, rates):
    fields = ctl.shape[0]
    tiles = coef.shape[1] // 8
    own_rates = (rate[0], masked_north(rate))
    for k in range(2):
        for row, block in blocks(own_rates[k], south[fields + k], north[fields + k]):
            rates[2 * k, pl.ds(row, block.shape[0]), :] = block
        for row, block in blocks(strip[...], south[fields + 2], north[fields + 2]):
            lane = lanes(block.shape)
            near = (lane < HALO) | (lane >= block.shape[-1] - HALO)
            rates[2 * k + 1, pl.ds(row, block.shape[0]), :] = jnp.where(
                near, unpack(block, fields + k), 0.0
            )
        clear = jnp.zeros((PAD, rates.shape[2]), F32)
        for plane in (2 * k, 2 * k + 1):
            rates[plane, pl.ds(0, PAD), :] = clear
    for tile in range(tiles):
        here, down = pl.ds(PAD + 8 * tile, 8), pl.ds(PAD + 8 * tile - 1, 8)
        east = (rates[0, here, :], rates[1, here, :])
        west = turned(east[0], east[1], 1)
        for plane in range(2):
            n, s = rates[2 + plane, here, :], rates[2 + plane, down, :]
            e, w = east[plane], west[plane]
            for i, value in enumerate((1.0 - e - w - n - s, e, w, n, s)):
                coef[2 * i + plane, pl.ds(8 * tile, 8), :] = value
    load_field(a, ctl, strip, south, north)

    def finish(f, row, main):
        inc[f, pl.ds(row, 8), :] = main

    ten_steps(a, b, coef, finish, tiles)


def diffuse_pulled(pulled, strip, south, north, coef, ctl, grad, a, b):
    load_field(a, pulled, strip, south, north)

    def finish(f, row, main):
        grad[f, pl.ds(row, 8), :] = ctl[f, pl.ds(row, 8), :] + main

    ten_steps(a, b, coef, finish, coef.shape[1] // 8)


def tables(obs, holder, cell, out, slots):
    profiles = holder.shape[1]
    level_here = lax.axis_index("obs")
    groups = obs.shape[0] // 16
    width = obs.shape[1]
    acc = jnp.zeros((48, profiles), F32)
    row16 = subs((16, width))
    for z in range(groups):
        parts = ([], [], [])
        hots = []
        for c in range(4):
            at = 16 * z + c
            index = obs[pl.ds(at, 1), :].astype(I32)
            w, y, q = (obs[pl.ds(at + 4 * k, 1), :] for k in (1, 2, 3))
            prof = index & 511
            level = (index >> 9) & 7
            field = index >> 12
            low = jnp.where(level == level_here, q, 0.0)
            high = jnp.where(level == level_here - 1, q, 0.0)
            v = 1.0 - w
            lw, hv = low * w, high * v
            rows = (lw * w + hv * v, lw * v, hv * w, (lw + hv) * y)
            value = jnp.where(
                row16 < 8,
                jnp.where(row16 < 4, rows[0], rows[1]),
                jnp.where(row16 < 12, rows[2], rows[3]),
            )
            value = jnp.where((row16 & 3) == field, value, 0.0)
            for part, x in zip(parts, split3(value)):
                part.append(x)
            hots.append(one_hot(subs((profiles, width)) == prof))
        left = jnp.concatenate([jnp.concatenate(p, axis=1) for p in parts], axis=0)
        acc = acc + dot_nt(left, jnp.concatenate(hots, axis=1))
    table = acc[0:16] + acc[16:32] + acc[32:48]
    held = subs((out.shape[0], profiles)) == holder[...]
    held16 = one_hot(held)
    before = one_hot(subs((profiles, profiles)) < lanes((profiles, profiles)))
    slot = jnp.sum(jnp.where(held, dot_nn(held16, before), 0.0), axis=0, keepdims=True)
    slots[...] = slot
    place = slot.astype(I32)
    cells = cell[...].astype(F32)
    mine = [subs((8, profiles)) * 2 + k == place for k in range(2)]
    for k in range(2):
        value = jnp.concatenate(
            [jnp.where(mine[k], table[r : r + 1], 0.0) for r in range(16)], axis=0
        )
        total = sum(dot_nt(held16, part) for part in split3(value))
        out[:, k, :] = total
    value = jnp.concatenate(
        [jnp.where(mine[k], cells, 0.0) for k in range(2)]
        + [jnp.zeros((112, profiles), F32)],
        axis=0,
    )
    out[:, 2, :] = sum(dot_nt(held16, part) for part in split3(value)[:2])


def gather(inc, sent, found, tab, hold):
    fields = inc.shape[0]
    tab[pl.ds(0, 128), :] = jnp.concatenate([sent[:, 0, :], sent[:, 1, :]], axis=0).T
    cells = jnp.concatenate([sent[:, 2, :], sent[:, 2, :]], axis=0).T
    cells = jnp.where(lanes((8, 128)) < 64, cells[0:8], cells[8:16])
    tab[pl.ds(128, 8), :] = cells
    cells = cells.astype(I32)
    left = jnp.concatenate(
        [jnp.concatenate(split3(inc[f]), axis=1) for f in range(fields)], axis=0
    )
    for pair in range(4):
        hots, lats = [], []
        for s in (2 * pair, 2 * pair + 1):
            row = cells[s : s + 1]
            hots.append(one_hot(subs((128, 128)) == (row & 127)))
            lats.append(subs((128, 128)) == (row >> 7))
        hot = jnp.concatenate(hots, axis=1)
        hit = dot_nn(left, jnp.concatenate([hot, hot, hot], axis=0))
        for f in range(fields):
            for i in range(2):
                part = hit[128 * f : 128 * (f + 1), 128 * i : 128 * (i + 1)]
                hold[pl.ds(8 * f + 2 * pair + i, 1), :] = jnp.sum(
                    jnp.where(lats[i], part, 0.0), axis=0, keepdims=True
                )
    rows = hold[...]
    for z in range(found.shape[0] // rows.shape[0]):
        found[pl.ds(z * rows.shape[0], rows.shape[0]), :] = rows


def scatter(levels, tab, pulled, east, west, columns):
    fields = pulled.shape[0]
    rows = 8 * fields
    here = lax.axis_index("obs")
    top = levels.shape[0] // rows - 1

    def level(k):
        return levels[pl.ds(pl.multiple_of(jnp.clip(k, 0, top) * rows, rows), rows), :]

    own, above, below = level(here), level(here + 1), level(here - 1)
    d, o, u, b = (tab[pl.ds(rows * k, rows), :] for k in range(4))
    amount = d * own + o * above + u * below - b
    cells = tab[pl.ds(4 * rows, 8), :].astype(I32)
    lat = [subs((128, 128)) == (cells[s : s + 1] >> 7) for s in range(8)]
    hot = jnp.concatenate(
        [one_hot(subs((128, 128)) == (cells[s : s + 1] & 127)) for s in range(8)], axis=1
    )
    for f in range(fields):
        total = jnp.zeros((128, 128), F32)
        for part in split3(amount[8 * f : 8 * f + 8]):
            wide = part.astype(F32)
            left = jnp.concatenate(
                [jnp.where(lat[s], wide[s : s + 1], 0.0).astype(BF16) for s in range(8)], axis=1
            )
            total = total + dot_nt(left, hot)
        pulled[f] = total
    pack_edges([pulled[f] for f in range(fields)], east, west)
    for half in range(2):
        turned_block = levels[pl.ds(128 * half, 128), :].T
        for k in range(2):
            columns[:, 2 * k + half, :] = turned_block[64 * k : 64 * (k + 1)]


def depart(columns, holder, slots, prof, field, level, weight, innov, prec, out):
    profiles = holder.shape[1]
    left = jnp.concatenate(
        [
            jnp.concatenate([columns[:, half, :], columns[:, 2 + half, :]], axis=0).T
            for half in range(2)
        ],
        axis=0,
    )
    place = slots[...].astype(I32)
    row = subs((128, profiles))
    held = one_hot(((row & 63) == holder[...]) & ((row >> 6) == (place & 1)))
    spread = dot_nn(
        jnp.concatenate(split3(left), axis=1), jnp.concatenate([held, held, held], axis=0)
    )
    mine = subs((8, profiles)) == (place >> 1)
    values = jnp.concatenate(
        [
            jnp.sum(jnp.where(mine, spread[8 * r : 8 * r + 8], 0.0), axis=0, keepdims=True)
            for r in range(32)
        ],
        axis=0,
    )
    hot = jnp.concatenate(
        [one_hot(subs((profiles, 128)) == prof[pl.ds(c, 1), :]) for c in range(4)], axis=1
    )
    seen = sum(dot_nn(part, hot) for part in split3(values))
    row = subs((32, 128))
    for c in range(4):
        at = pl.ds(c, 1)
        code = level[at, :] * 4 + field[at, :]
        part = seen[:, 128 * c : 128 * (c + 1)]
        low = jnp.sum(jnp.where(row == code, part, 0.0), axis=0, keepdims=True)
        high = jnp.sum(jnp.where(row == code + 4, part, 0.0), axis=0, keepdims=True)
        w = weight[at, :]
        out[at, :] = prec[at, :] * (w * low + (1.0 - w) * high - innov[at, :])


def ring(axis, by):
    count = lax.axis_size(axis)
    return [(i, (i + by) % count) for i in range(count)]


def pair(forward, back, axis):
    return (
        lax.ppermute(forward, axis, ring(axis, 1)),
        lax.ppermute(back, axis, ring(axis, -1)),
    )


def per_device(
    control,
    diffusivity,
    prof_tile,
    prof_cell,
    obs_prof,
    obs_field,
    obs_level,
    obs_weight,
    innovation,
    obs_precision,
):
    fields, _, ny, nx = control.shape
    tile = (ny, nx)
    profiles = prof_tile.shape[0]
    holders = lax.axis_size("gx") * lax.axis_size("gy")
    levels = lax.axis_size("obs")
    ext = ny + 2 * ROWS
    ctl = control.reshape(fields, ny, nx)
    rate = diffusivity.reshape(2, ny, nx)
    holder = prof_tile.reshape(1, profiles)
    cell = prof_cell.reshape(1, profiles)
    obs = [
        x.reshape(4, 128)
        for x in (obs_prof, obs_field, obs_level, obs_weight, innovation, obs_precision)
    ]
    planes = pltpu.VMEM((2 * fields, ext + 2 * PAD, nx), F32)

    east, west, rows = call(pack_inputs, [tile, tile, (levels * 16, 128)], [ctl, rate, *obs])
    rows = lax.all_to_all(rows, "obs", 0, 0, tiled=True)
    left, right = pair(east, west, "gx")
    side = (fields + 3, ROWS, nx)
    strip, north, south = call(edges_first, [tile, side, side], [ctl, rate, left, right])
    south, north = pair(north, south, "gy")
    table, slots = call(
        tables, [(holders, 3, 128), (1, profiles)], [rows, holder, cell], flops=400_000_000
    )
    table = lax.all_to_all(table, ("gx", "gy"), 0, 0, tiled=True)
    inc, coef = call(
        diffuse_control,
        [(fields, ny, nx), (10, ext, nx)],
        [ctl, rate, strip, south, north],
        [planes, planes, pltpu.VMEM((4, ext + 2 * PAD, nx), F32)],
        flops=40_000_000,
    )
    found, tab = call(
        gather,
        [(levels * fields * 8, 128), (136, 128)],
        [inc, table],
        [pltpu.VMEM((fields * 8, 128), F32)],
        flops=400_000_000,
    )
    found = lax.all_to_all(found, "obs", 0, 0, tiled=True)
    pulled, east, west, columns = call(
        scatter,
        [(fields, ny, nx), tile, tile, (holders, 4, 128)],
        [found, tab],
        flops=400_000_000,
    )
    left, right = pair(east, west, "gx")
    columns = lax.all_to_all(columns, ("gx", "gy"), 0, 0, tiled=True)
    side = (fields + 1, ROWS, nx)
    strip, north, south = call(edges_second, [tile, side, side], [pulled, left, right])
    south, north = pair(north, south, "gy")
    (gradient,) = call(
        diffuse_pulled,
        [(fields, ny, nx)],
        [pulled, strip, south, north, coef, ctl],
        [planes, planes],
        flops=40_000_000,
    )
    (departures,) = call(depart, [(4, 128)], [columns, holder, slots, *obs], flops=400_000_000)
    return gradient.reshape(control.shape), departures.reshape(obs_prof.shape)


def solution(mesh):
    in_specs = (
        P(None, "obs", "gy", "gx"),
        P(None, "obs", "gy", "gx"),
        P(("gx", "gy"), None),
        P(("gx", "gy")),
        P(("gx", "gy", "obs")),
        P(("gx", "gy", "obs")),
        P(("gx", "gy", "obs")),
        P(("gx", "gy", "obs")),
        P(("gx", "gy", "obs")),
        P(("gx", "gy", "obs")),
    )
    out_specs = (P(None, "obs", "gy", "gx"), P(("gx", "gy", "obs")))
    return jax.shard_map(
        per_device, mesh=mesh, in_specs=in_specs, out_specs=out_specs, check_vma=False
    )
```

```python
import jax
import jax.numpy as jnp
from jax import lax
from jax.experimental import pallas as pl
from jax.experimental.pallas import tpu as pltpu
from jax.sharding import PartitionSpec as P

STEPS = 10
HALO = STEPS
ROWS = 16
PITCH = 2 * HALO
PAD = 8
F32, BF16, I32 = jnp.float32, jnp.bfloat16, jnp.int32


def lanes(shape):
    return lax.broadcasted_iota(I32, shape, len(shape) - 1)


def subs(shape):
    return lax.broadcasted_iota(I32, shape, len(shape) - 2)


def split3(x):
    hi = x.astype(BF16)
    rest = x - hi.astype(F32)
    mid = rest.astype(BF16)
    low = (rest - mid.astype(F32)).astype(BF16)
    return hi, mid, low


def one_hot(flags):
    return jnp.where(flags, 1.0, 0.0).astype(BF16)


def dot_nn(a, b):
    return lax.dot_general(a, b, (((1,), (0,)), ((), ())), preferred_element_type=F32)


def dot_nt(a, b):
    return lax.dot_general(a, b, (((1,), (1,)), ((), ())), preferred_element_type=F32)


def call(body, outs, args, scratch=(), flops=1_000_000, smem=()):
    vmem = pl.BlockSpec(memory_space=pltpu.VMEM)
    moved = sum(a.size * 4 for a in args) + sum(4 * _size(s) for s in outs)
    return pl.pallas_call(
        body,
        out_shape=[jax.ShapeDtypeStruct(s, F32) for s in outs],
        in_specs=[vmem] * len(args),
        out_specs=[vmem] * len(outs),
        scratch_shapes=list(scratch),
        cost_estimate=pl.CostEstimate(flops=flops, bytes_accessed=moved, transcendentals=0),
        compiler_params=pltpu.CompilerParams(vmem_limit_bytes=16 << 20),
        name=body.__name__,
    )(*args)


def _size(shape):
    n = 1
    for s in shape:
        n *= s
    return n


def masked_north(rate_ref):
    north = rate_ref[1]
    top = lax.axis_index("gy") == lax.axis_size("gy") - 1
    return jnp.where(top & (subs(north.shape) == north.shape[0] - 1), 0.0, north)


def pack_edges(arrays, east_ref, west_ref):
    lane = lanes(arrays[0].shape)
    east = jnp.zeros(arrays[0].shape, F32)
    west = jnp.zeros(arrays[0].shape, F32)
    for a, x in enumerate(arrays):
        width = x.shape[-1]
        low = a * PITCH + HALO
        moved = pltpu.roll(x, (low - (width - HALO)) % width, 1)
        east = jnp.where((lane >= low) & (lane < low + HALO), moved, east)
        low = a * PITCH
        moved = pltpu.roll(x, low % width, 1) if low else x
        west = jnp.where((lane >= low) & (lane < low + HALO), moved, west)
    east_ref[...] = east
    west_ref[...] = west


def pack_inputs(ctl, rate, prof, field, level, weight, innov, prec, east, west, obs):
    pack_edges([ctl[f] for f in range(ctl.shape[0])] + [rate[0], masked_north(rate)], east, west)
    index = ((field[...] * 8 + level[...]) * 512 + prof[...]).astype(F32)
    rows = jnp.concatenate([index, weight[...], innov[...], prec[...]], axis=0)
    for z in range(obs.shape[0] // rows.shape[0]):
        obs[pl.ds(z * rows.shape[0], rows.shape[0]), :] = rows


def north_south(arrays, strip, north_ref, south_ref):
    for a, x in enumerate(arrays + [strip]):
        north_ref[a] = x[x.shape[0] - ROWS :]
        south_ref[a] = x[:ROWS]


def edges_first(ctl, rate, left, right, strip, north, south):
    joined = left[...] + right[...]
    strip[...] = joined
    arrays = [ctl[f] for f in range(ctl.shape[0])] + [rate[0], masked_north(rate)]
    north_south(arrays, joined, north, south)


def edges_second(pulled, left, right, strip, north, south):
    joined = left[...] + right[...]
    strip[...] = joined
    north_south([pulled[f] for f in range(pulled.shape[0])], joined, north, south)


def unpack(block, a):
    width = block.shape[-1]
    east = pltpu.roll(block, (-a * PITCH) % width, 1) if a else block
    west = pltpu.roll(block, (width - HALO - a * PITCH - HALO) % width, 1)
    return jnp.where(lanes(block.shape) < width // 2, east, west)


def blocks(own, south, north):
    height = own.shape[0]
    return ((PAD, south), (PAD + ROWS, own), (PAD + ROWS + height, north))


def turned(main, beyond, by):
    width = main.shape[-1]
    edge = lanes(main.shape) == (0 if by == 1 else width - 1)
    a = pltpu.roll(main, by % width, 1)
    b = pltpu.roll(beyond, by % width, 1)
    return jnp.where(edge, b, a), jnp.where(edge, a, b)


def one_step(source, coef, store, first, last):
    fields = source.shape[0] // 2
    for tile in range(first, last):
        row = PAD + 8 * tile
        here, up, down = pl.ds(row, 8), pl.ds(row + 1, 8), pl.ds(row - 1, 8)
        c = [coef[i, pl.ds(8 * tile, 8), :] for i in range(10)]
        for f in range(fields):
            m, s = source[2 * f, here, :], source[2 * f + 1, here, :]
            me, se = turned(m, s, -1)
            mw, sw = turned(m, s, 1)
            new_m = c[0] * m + c[2] * me + c[4] * mw + c[6] * source[2 * f, up, :]
            new_m = new_m + c[8] * source[2 * f, down, :]
            new_s = c[1] * s + c[3] * se + c[5] * sw + c[7] * source[2 * f + 1, up, :]
            new_s = new_s + c[9] * source[2 * f + 1, down, :]
            store(f, tile, new_m, new_s)


def ten_steps(a, b, coef, finish, tiles):
    def into(target):
        def store(f, tile, main, beyond):
            target[2 * f, pl.ds(PAD + 8 * tile, 8), :] = main
            target[2 * f + 1, pl.ds(PAD + 8 * tile, 8), :] = beyond

        return store

    one_step(a, coef, into(b), 0, tiles)

    def body(_, carry):
        one_step(b, coef, into(a), 1, tiles - 1)
        one_step(a, coef, into(b), 1, tiles - 1)
        return carry

    lax.fori_loop(0, STEPS // 2 - 1, body, 0)

    def store(f, tile, main, beyond):
        finish(f, 8 * tile - ROWS, main)

    one_step(b, coef, store, ROWS // 8, tiles - ROWS // 8)


def load_field(a, own, strip, south, north):
    fields = own.shape[0]
    for f in range(fields):
        for row, block in blocks(own[f], south[f], north[f]):
            a[2 * f, pl.ds(row, block.shape[0]), :] = block
    for row, block in blocks(strip[...], south[south.shape[0] - 1], north[north.shape[0] - 1]):
        for f in range(fields):
            a[2 * f + 1, pl.ds(row, block.shape[0]), :] = unpack(block, f)
    clear = jnp.zeros((PAD, a.shape[2]), F32)
    for plane in range(a.shape[0]):
        a[plane, pl.ds(0, PAD), :] = clear
        a[plane, pl.ds(a.shape[1] - PAD, PAD), :] = clear


def diffuse_control(ctl, rate, strip, south, north, inc, coef, a, b, rates):
    fields = ctl.shape[0]
    tiles = coef.shape[1] // 8
    own_rates = (rate[0], masked_north(rate))
    for k in range(2):
        for row, block in blocks(own_rates[k], south[fields + k], north[fields + k]):
            rates[2 * k, pl.ds(row, block.shape[0]), :] = block
        for row, block in blocks(strip[...], south[fields + 2], north[fields + 2]):
            lane = lanes(block.shape)
            near = (lane < HALO) | (lane >= block.shape[-1] - HALO)
            rates[2 * k + 1, pl.ds(row, block.shape[0]), :] = jnp.where(
                near, unpack(block, fields + k), 0.0
            )
        clear = jnp.zeros((PAD, rates.shape[2]), F32)
        for plane in (2 * k, 2 * k + 1):
            rates[plane, pl.ds(0, PAD), :] = clear
    for tile in range(tiles):
        here, down = pl.ds(PAD + 8 * tile, 8), pl.ds(PAD + 8 * tile - 1, 8)
        east = (rates[0, here, :], rates[1, here, :])
        west = turned(east[0], east[1], 1)
        for plane in range(2):
            n, s = rates[2 + plane, here, :], rates[2 + plane, down, :]
            e, w = east[plane], west[plane]
            for i, value in enumerate((1.0 - e - w - n - s, e, w, n, s)):
                coef[2 * i + plane, pl.ds(8 * tile, 8), :] = value
    load_field(a, ctl, strip, south, north)

    def finish(f, row, main):
        inc[f, pl.ds(row, 8), :] = main

    ten_steps(a, b, coef, finish, tiles)


def diffuse_pulled(pulled, strip, south, north, coef, ctl, grad, a, b):
    load_field(a, pulled, strip, south, north)

    def finish(f, row, main):
        grad[f, pl.ds(row, 8), :] = ctl[f, pl.ds(row, 8), :] + main

    ten_steps(a, b, coef, finish, coef.shape[1] // 8)


def tables(obs, holder, cell, out, slots):
    profiles = holder.shape[1]
    level_here = lax.axis_index("obs")
    groups = obs.shape[0] // 16
    width = obs.shape[1]
    acc = jnp.zeros((48, profiles), F32)
    row16 = subs((16, width))
    for z in range(groups):
        parts = ([], [], [])
        hots = []
        for c in range(4):
            at = 16 * z + c
            index = obs[pl.ds(at, 1), :].astype(I32)
            w, y, q = (obs[pl.ds(at + 4 * k, 1), :] for k in (1, 2, 3))
            prof = index & 511
            level = (index >> 9) & 7
            field = index >> 12
            low = jnp.where(level == level_here, q, 0.0)
            high = jnp.where(level == level_here - 1, q, 0.0)
            v = 1.0 - w
            lw, hv = low * w, high * v
            rows = (lw * w + hv * v, lw * v, hv * w, (lw + hv) * y)
            value = jnp.where(
                row16 < 8,
                jnp.where(row16 < 4, rows[0], rows[1]),
                jnp.where(row16 < 12, rows[2], rows[3]),
            )
            value = jnp.where((row16 & 3) == field, value, 0.0)
            for part, x in zip(parts, split3(value)):
                part.append(x)
            hots.append(one_hot(subs((profiles, width)) == prof))
        left = jnp.concatenate([jnp.concatenate(p, axis=1) for p in parts], axis=0)
        acc = acc + dot_nt(left, jnp.concatenate(hots, axis=1))
    table = acc[0:16] + acc[16:32] + acc[32:48]
    held = subs((out.shape[0], profiles)) == holder[...]
    held16 = one_hot(held)
    before = one_hot(subs((profiles, profiles)) < lanes((profiles, profiles)))
    slot = jnp.sum(jnp.where(held, dot_nn(held16, before), 0.0), axis=0, keepdims=True)
    slots[...] = slot
    place = slot.astype(I32)
    cells = cell[...].astype(F32)
    mine = [subs((8, profiles)) * 2 + k == place for k in range(2)]
    for k in range(2):
        value = jnp.concatenate(
            [jnp.where(mine[k], table[r : r + 1], 0.0) for r in range(16)], axis=0
        )
        total = sum(dot_nt(held16, part) for part in split3(value))
        out[:, k, :] = total
    value = jnp.concatenate(
        [jnp.where(mine[k], cells, 0.0) for k in range(2)]
        + [jnp.zeros((112, profiles), F32)],
        axis=0,
    )
    out[:, 2, :] = sum(dot_nt(held16, part) for part in split3(value)[:2])


def gather(inc, sent, found, tab, hold):
    fields = inc.shape[0]
    tab[pl.ds(0, 128), :] = jnp.concatenate([sent[:, 0, :], sent[:, 1, :]], axis=0).T
    cells = jnp.concatenate([sent[:, 2, :], sent[:, 2, :]], axis=0).T
    cells = jnp.where(lanes((8, 128)) < 64, cells[0:8], cells[8:16])
    tab[pl.ds(128, 8), :] = cells
    cells = cells.astype(I32)
    left = jnp.concatenate(
        [jnp.concatenate(split3(inc[f]), axis=1) for f in range(fields)], axis=0
    )
    for pair in range(4):
        hots, lats = [], []
        for s in (2 * pair, 2 * pair + 1):
            row = cells[s : s + 1]
            hots.append(one_hot(subs((128, 128)) == (row & 127)))
            lats.append(subs((128, 128)) == (row >> 7))
        hot = jnp.concatenate(hots, axis=1)
        hit = dot_nn(left, jnp.concatenate([hot, hot, hot], axis=0))
        for f in range(fields):
            for i in range(2):
                part = hit[128 * f : 128 * (f + 1), 128 * i : 128 * (i + 1)]
                hold[pl.ds(8 * f + 2 * pair + i, 1), :] = jnp.sum(
                    jnp.where(lats[i], part, 0.0), axis=0, keepdims=True
                )
    rows = hold[...]
    for z in range(found.shape[0] // rows.shape[0]):
        found[pl.ds(z * rows.shape[0], rows.shape[0]), :] = rows


def scatter(levels, tab, pulled, east, west, columns):
    fields = pulled.shape[0]
    rows = 8 * fields
    here = lax.axis_index("obs")
    top = levels.shape[0] // rows - 1

    def level(k):
        return levels[pl.ds(pl.multiple_of(jnp.clip(k, 0, top) * rows, rows), rows), :]

    own, above, below = level(here), level(here + 1), level(here - 1)
    d, o, u, b = (tab[pl.ds(rows * k, rows), :] for k in range(4))
    amount = d * own + o * above + u * below - b
    cells = tab[pl.ds(4 * rows, 8), :].astype(I32)
    lat = [subs((128, 128)) == (cells[s : s + 1] >> 7) for s in range(8)]
    hot = jnp.concatenate(
        [one_hot(subs((128, 128)) == (cells[s : s + 1] & 127)) for s in range(8)], axis=1
    )
    for f in range(fields):
        total = jnp.zeros((128, 128), F32)
        for part in split3(amount[8 * f : 8 * f + 8]):
            wide = part.astype(F32)
            left = jnp.concatenate(
                [jnp.where(lat[s], wide[s : s + 1], 0.0).astype(BF16) for s in range(8)], axis=1
            )
            total = total + dot_nt(left, hot)
        pulled[f] = total
    pack_edges([pulled[f] for f in range(fields)], east, west)
    for half in range(2):
        turned_block = levels[pl.ds(128 * half, 128), :].T
        for k in range(2):
            columns[:, 2 * k + half, :] = turned_block[64 * k : 64 * (k + 1)]


def depart(columns, holder, slots, prof, field, level, weight, innov, prec, out):
    profiles = holder.shape[1]
    left = jnp.concatenate(
        [
            jnp.concatenate([columns[:, half, :], columns[:, 2 + half, :]], axis=0).T
            for half in range(2)
        ],
        axis=0,
    )
    place = slots[...].astype(I32)
    row = subs((128, profiles))
    held = one_hot(((row & 63) == holder[...]) & ((row >> 6) == (place & 1)))
    spread = dot_nn(
        jnp.concatenate(split3(left), axis=1), jnp.concatenate([held, held, held], axis=0)
    )
    mine = subs((8, profiles)) == (place >> 1)
    values = jnp.concatenate(
        [
            jnp.sum(jnp.where(mine, spread[8 * r : 8 * r + 8], 0.0), axis=0, keepdims=True)
            for r in range(32)
        ],
        axis=0,
    )
    hot = jnp.concatenate(
        [one_hot(subs((profiles, 128)) == prof[pl.ds(c, 1), :]) for c in range(4)], axis=1
    )
    seen = sum(dot_nn(part, hot) for part in split3(values))
    row = subs((32, 128))
    for c in range(4):
        at = pl.ds(c, 1)
        code = level[at, :] * 4 + field[at, :]
        part = seen[:, 128 * c : 128 * (c + 1)]
        low = jnp.sum(jnp.where(row == code, part, 0.0), axis=0, keepdims=True)
        high = jnp.sum(jnp.where(row == code + 4, part, 0.0), axis=0, keepdims=True)
        w = weight[at, :]
        out[at, :] = prec[at, :] * (w * low + (1.0 - w) * high - innov[at, :])


def ring(axis, by):
    count = lax.axis_size(axis)
    return [(i, (i + by) % count) for i in range(count)]


def pair(forward, back, axis):
    return (
        lax.ppermute(forward, axis, ring(axis, 1)),
        lax.ppermute(back, axis, ring(axis, -1)),
    )


def per_device(
    control,
    diffusivity,
    prof_tile,
    prof_cell,
    obs_prof,
    obs_field,
    obs_level,
    obs_weight,
    innovation,
    obs_precision,
):
    fields, _, ny, nx = control.shape
    tile = (ny, nx)
    profiles = prof_tile.shape[0]
    holders = lax.axis_size("gx") * lax.axis_size("gy")
    levels = lax.axis_size("obs")
    ext = ny + 2 * ROWS
    ctl = control.reshape(fields, ny, nx)
    rate = diffusivity.reshape(2, ny, nx)
    holder = prof_tile.reshape(1, profiles)
    cell = prof_cell.reshape(1, profiles)
    obs = [
        x.reshape(4, 128)
        for x in (obs_prof, obs_field, obs_level, obs_weight, innovation, obs_precision)
    ]
    planes = pltpu.VMEM((2 * fields, ext + 2 * PAD, nx), F32)

    east, west, rows = call(pack_inputs, [tile, tile, (levels * 16, 128)], [ctl, rate, *obs])
    rows = lax.all_to_all(rows, "obs", 0, 0, tiled=True)
    left, right = pair(east, west, "gx")
    side = (fields + 3, ROWS, nx)
    strip, north, south = call(edges_first, [tile, side, side], [ctl, rate, left, right])
    south, north = pair(north, south, "gy")
    table, slots = call(
        tables, [(holders, 3, 128), (1, profiles)], [rows, holder, cell], flops=400_000_000
    )
    table = lax.all_to_all(table, ("gx", "gy"), 0, 0, tiled=True)
    inc, coef = call(
        diffuse_control,
        [(fields, ny, nx), (10, ext, nx)],
        [ctl, rate, strip, south, north],
        [planes, planes, pltpu.VMEM((4, ext + 2 * PAD, nx), F32)],
        flops=40_000_000,
    )
    found, tab = call(
        gather,
        [(levels * fields * 8, 128), (136, 128)],
        [inc, table],
        [pltpu.VMEM((fields * 8, 128), F32)],
        flops=400_000_000,
    )
    found = lax.all_to_all(found, "obs", 0, 0, tiled=True)
    pulled, east, west, columns = call(
        scatter,
        [(fields, ny, nx), tile, tile, (holders, 4, 128)],
        [found, tab],
        flops=400_000_000,
    )
    left, right = pair(east, west, "gx")
    columns = lax.all_to_all(columns, ("gx", "gy"), 0, 0, tiled=True)
    side = (fields + 1, ROWS, nx)
    strip, north, south = call(edges_second, [tile, side, side], [pulled, left, right])
    south, north = pair(north, south, "gy")
    (gradient,) = call(
        diffuse_pulled,
        [(fields, ny, nx)],
        [pulled, strip, south, north, coef, ctl],
        [planes, planes],
        flops=40_000_000,
    )
    (departures,) = call(depart, [(4, 128)], [columns, holder, slots, *obs], flops=400_000_000)
    return gradient.reshape(control.shape), departures.reshape(obs_prof.shape)


def solution(mesh):
    in_specs = (
        P(None, "obs", "gy", "gx"),
        P(None, "obs", "gy", "gx"),
        P(("gx", "gy"), None),
        P(("gx", "gy")),
        P(("gx", "gy", "obs")),
        P(("gx", "gy", "obs")),
        P(("gx", "gy", "obs")),
        P(("gx", "gy", "obs")),
        P(("gx", "gy", "obs")),
        P(("gx", "gy", "obs")),
    )
    out_specs = (P(None, "obs", "gy", "gx"), P(("gx", "gy", "obs")))
    return jax.shard_map(
        per_device, mesh=mesh, in_specs=in_specs, out_specs=out_specs, check_vma=False
    )
```

```python
import jax
import jax.numpy as jnp
from jax import lax
from jax.experimental import pallas as pl
from jax.experimental.pallas import tpu as pltpu
from jax.sharding import PartitionSpec as P


STEPS = 10
HALO = STEPS
ROWS = 16
PITCH = 2 * HALO
PAD = 8
F32, BF16, I32 = jnp.float32, jnp.bfloat16, jnp.int32


def lanes(shape):
    return lax.broadcasted_iota(I32, shape, len(shape) - 1)


def subs(shape):
    return lax.broadcasted_iota(I32, shape, len(shape) - 2)


def split3(x):
    hi = x.astype(BF16)
    rest = x - hi.astype(F32)
    mid = rest.astype(BF16)
    low = (rest - mid.astype(F32)).astype(BF16)
    return hi, mid, low


def one_hot(flags):
    return jnp.where(flags, 1.0, 0.0).astype(BF16)


def dot_nn(a, b):
    return lax.dot_general(a, b, (((1,), (0,)), ((), ())), preferred_element_type=F32)


def dot_nt(a, b):
    return lax.dot_general(a, b, (((1,), (1,)), ((), ())), preferred_element_type=F32)


def call(body, outs, args, scratch=(), flops=1_000_000, hbm=False):
    vmem = pl.BlockSpec(memory_space=pltpu.VMEM)
    given = pl.BlockSpec(memory_space=pltpu.HBM) if hbm else vmem
    outs = [o if isinstance(o, jax.ShapeDtypeStruct) else jax.ShapeDtypeStruct(o, F32) for o in outs]
    return pl.pallas_call(
        body,
        out_shape=outs,
        in_specs=[given] * len(args),
        out_specs=[vmem] * len(outs),
        scratch_shapes=list(scratch),
        cost_estimate=pl.CostEstimate(
            flops=flops,
            bytes_accessed=sum(4 * x.size for x in (*args, *outs)),
            transcendentals=0,
        ),
        compiler_params=pltpu.CompilerParams(vmem_limit_bytes=16 << 20),
    )(*args)


def mask_north(rate_ref):
    last = rate_ref.shape[1] - 8
    rows = rate_ref[1, pl.ds(last, 8), :]
    top = lax.axis_index("gy") == lax.axis_size("gy") - 1
    rate_ref[1, pl.ds(last, 8), :] = jnp.where(top & (subs(rows.shape) == 7), 0.0, rows)


def pack_edges(arrays, east_ref, west_ref):
    lane = lanes(arrays[0].shape)
    east = jnp.zeros(arrays[0].shape, F32)
    west = jnp.zeros(arrays[0].shape, F32)
    for a, x in enumerate(arrays):
        width = x.shape[-1]
        low = a * PITCH + HALO
        moved = pltpu.roll(x, (low - (width - HALO)) % width, 1)
        east = jnp.where((lane >= low) & (lane < low + HALO), moved, east)
        low = a * PITCH
        moved = pltpu.roll(x, low % width, 1) if low else x
        west = jnp.where((lane >= low) & (lane < low + HALO), moved, west)
    east_ref[...] = east
    west_ref[...] = west


def pack_inputs(*refs):
    sources, (east, west, obs), kept, sems = refs[:10], refs[10:13], refs[13:23], refs[23]
    copies = [
        pltpu.make_async_copy(source, target, sems.at[i])
        for i, (source, target) in enumerate(zip(sources, kept))
    ]
    for copy in copies:
        copy.start()
    for copy in copies:
        copy.wait()
    ctl, rate, _, _, prof, field, level, weight, innov, prec = kept
    mask_north(rate)
    pack_edges([ctl[f] for f in range(ctl.shape[0])] + [rate[0], rate[1]], east, west)
    index = ((field[...] * 8 + level[...]) * 512 + prof[...]).astype(F32)
    rows = jnp.concatenate([index, weight[...], innov[...], prec[...]], axis=0)
    for z in range(obs.shape[0] // rows.shape[0]):
        obs[pl.ds(z * rows.shape[0], rows.shape[0]), :] = rows


def north_south(arrays, strip, north_ref, south_ref):
    for a, x in enumerate(arrays + [strip]):
        north_ref[a] = x[x.shape[0] - ROWS :]
        south_ref[a] = x[:ROWS]


def edges_first(ctl, rate, left, right, strip, north, south):
    joined = left[...] + right[...]
    strip[...] = joined
    arrays = [ctl[f] for f in range(ctl.shape[0])] + [rate[0], rate[1]]
    north_south(arrays, joined, north, south)


def edges_second(pulled, left, right, strip, north, south):
    joined = left[...] + right[...]
    strip[...] = joined
    north_south([pulled[f] for f in range(pulled.shape[0])], joined, north, south)


def unpack(block, a):
    width = block.shape[-1]
    east = pltpu.roll(block, (-a * PITCH) % width, 1) if a else block
    west = pltpu.roll(block, (width - HALO - a * PITCH - HALO) % width, 1)
    return jnp.where(lanes(block.shape) < width // 2, east, west)


def blocks(own, south, north):
    height = own.shape[0]
    return ((PAD, south), (PAD + ROWS, own), (PAD + ROWS + height, north))


def turned(main, beyond, by):
    width = main.shape[-1]
    edge = lanes(main.shape) == (0 if by == 1 else width - 1)
    a = pltpu.roll(main, by % width, 1)
    b = pltpu.roll(beyond, by % width, 1)
    return jnp.where(edge, b, a), jnp.where(edge, a, b)


def one_step(source, coef, store, first, last):
    fields = source.shape[0] // 2
    for tile in range(first, last):
        row = PAD + 8 * tile
        here, up, down = pl.ds(row, 8), pl.ds(row + 1, 8), pl.ds(row - 1, 8)
        c = [coef[i, pl.ds(8 * tile, 8), :] for i in range(10)]
        for f in range(fields):
            m, s = source[2 * f, here, :], source[2 * f + 1, here, :]
            me, se = turned(m, s, -1)
            mw, sw = turned(m, s, 1)
            new_m = c[0] * m + c[2] * me + c[4] * mw + c[6] * source[2 * f, up, :]
            new_m = new_m + c[8] * source[2 * f, down, :]
            new_s = c[1] * s + c[3] * se + c[5] * sw + c[7] * source[2 * f + 1, up, :]
            new_s = new_s + c[9] * source[2 * f + 1, down, :]
            store(f, tile, new_m, new_s)


def ten_steps(a, b, coef, finish, tiles):
    def into(target):
        def store(f, tile, main, beyond):
            target[2 * f, pl.ds(PAD + 8 * tile, 8), :] = main
            target[2 * f + 1, pl.ds(PAD + 8 * tile, 8), :] = beyond

        return store

    one_step(a, coef, into(b), 0, tiles)

    def body(_, carry):
        one_step(b, coef, into(a), 1, tiles - 1)
        one_step(a, coef, into(b), 1, tiles - 1)
        return carry

    lax.fori_loop(0, STEPS // 2 - 1, body, 0)

    def store(f, tile, main, beyond):
        finish(f, 8 * tile - ROWS, main)

    one_step(b, coef, store, ROWS // 8, tiles - ROWS // 8)


def load_field(a, own, strip, south, north):
    fields = own.shape[0]
    for f in range(fields):
        for row, block in blocks(own[f], south[f], north[f]):
            a[2 * f, pl.ds(row, block.shape[0]), :] = block
    for row, block in blocks(strip[...], south[south.shape[0] - 1], north[north.shape[0] - 1]):
        for f in range(fields):
            a[2 * f + 1, pl.ds(row, block.shape[0]), :] = unpack(block, f)
    clear = jnp.zeros((PAD, a.shape[2]), F32)
    for plane in range(a.shape[0]):
        a[plane, pl.ds(0, PAD), :] = clear
        a[plane, pl.ds(a.shape[1] - PAD, PAD), :] = clear


def diffuse_control(ctl, rate, strip, south, north, inc, coef, a, b, rates):
    fields = ctl.shape[0]
    tiles = coef.shape[1] // 8
    own_rates = (rate[0], rate[1])
    for k in range(2):
        for row, block in blocks(own_rates[k], south[fields + k], north[fields + k]):
            rates[2 * k, pl.ds(row, block.shape[0]), :] = block
        for row, block in blocks(strip[...], south[fields + 2], north[fields + 2]):
            lane = lanes(block.shape)
            near = (lane < HALO) | (lane >= block.shape[-1] - HALO)
            rates[2 * k + 1, pl.ds(row, block.shape[0]), :] = jnp.where(
                near, unpack(block, fields + k), 0.0
            )
        clear = jnp.zeros((PAD, rates.shape[2]), F32)
        for plane in (2 * k, 2 * k + 1):
            rates[plane, pl.ds(0, PAD), :] = clear
    for tile in range(tiles):
        here, down = pl.ds(PAD + 8 * tile, 8), pl.ds(PAD + 8 * tile - 1, 8)
        east = (rates[0, here, :], rates[1, here, :])
        west = turned(east[0], east[1], 1)
        for plane in range(2):
            n, s = rates[2 + plane, here, :], rates[2 + plane, down, :]
            e, w = east[plane], west[plane]
            for i, value in enumerate((1.0 - e - w - n - s, e, w, n, s)):
                coef[2 * i + plane, pl.ds(8 * tile, 8), :] = value
    load_field(a, ctl, strip, south, north)

    def finish(f, row, main):
        inc[f, pl.ds(row, 8), :] = main

    ten_steps(a, b, coef, finish, tiles)


def diffuse_pulled(pulled, strip, south, north, coef, ctl, grad, a, b):
    load_field(a, pulled, strip, south, north)

    def finish(f, row, main):
        grad[f, pl.ds(row, 8), :] = ctl[f, pl.ds(row, 8), :] + main

    ten_steps(a, b, coef, finish, coef.shape[1] // 8)


def tables(obs, holder, cell, out, slots):
    profiles = holder.shape[1]
    level_here = lax.axis_index("obs")
    groups = obs.shape[0] // 16
    width = obs.shape[1]
    acc = jnp.zeros((48, profiles), F32)
    row16 = subs((16, width))
    for z in range(groups):
        parts = ([], [], [])
        hots = []
        for c in range(4):
            at = 16 * z + c
            index = obs[pl.ds(at, 1), :].astype(I32)
            w, y, q = (obs[pl.ds(at + 4 * k, 1), :] for k in (1, 2, 3))
            prof = index & 511
            level = (index >> 9) & 7
            field = index >> 12
            low = jnp.where(level == level_here, q, 0.0)
            high = jnp.where(level == level_here - 1, q, 0.0)
            v = 1.0 - w
            lw, hv = low * w, high * v
            rows = (lw * w + hv * v, lw * v, hv * w, (lw + hv) * y)
            value = jnp.where(
                row16 < 8,
                jnp.where(row16 < 4, rows[0], rows[1]),
                jnp.where(row16 < 12, rows[2], rows[3]),
            )
            value = jnp.where((row16 & 3) == field, value, 0.0)
            for part, x in zip(parts, split3(value)):
                part.append(x)
            hots.append(one_hot(subs((profiles, width)) == prof))
        left = jnp.concatenate([jnp.concatenate(p, axis=1) for p in parts], axis=0)
        acc = acc + dot_nt(left, jnp.concatenate(hots, axis=1))
    table = acc[0:16] + acc[16:32] + acc[32:48]
    held = subs((out.shape[0], profiles)) == holder[...]
    held16 = one_hot(held)
    before = one_hot(subs((profiles, profiles)) < lanes((profiles, profiles)))
    slot = jnp.sum(jnp.where(held, dot_nn(held16, before), 0.0), axis=0, keepdims=True)
    slots[...] = slot
    place = slot.astype(I32)
    cells = cell[...].astype(F32)
    mine = [subs((8, profiles)) * 2 + k == place for k in range(2)]
    for k in range(2):
        value = jnp.concatenate(
            [jnp.where(mine[k], table[r : r + 1], 0.0) for r in range(16)], axis=0
        )
        total = sum(dot_nt(held16, part) for part in split3(value))
        out[:, k, :] = total
    value = jnp.concatenate(
        [jnp.where(mine[k], cells, 0.0) for k in range(2)]
        + [jnp.zeros((112, profiles), F32)],
        axis=0,
    )
    out[:, 2, :] = sum(dot_nt(held16, part) for part in split3(value)[:2])


def gather(inc, sent, found, tab, hold):
    fields = inc.shape[0]
    tab[pl.ds(0, 128), :] = jnp.concatenate([sent[:, 0, :], sent[:, 1, :]], axis=0).T
    cells = jnp.concatenate([sent[:, 2, :], sent[:, 2, :]], axis=0).T
    cells = jnp.where(lanes((8, 128)) < 64, cells[0:8], cells[8:16])
    tab[pl.ds(128, 8), :] = cells
    cells = cells.astype(I32)
    left = jnp.concatenate(
        [jnp.concatenate(split3(inc[f]), axis=1) for f in range(fields)], axis=0
    )
    for pair in range(4):
        hots, lats = [], []
        for s in (2 * pair, 2 * pair + 1):
            row = cells[s : s + 1]
            hots.append(one_hot(subs((128, 128)) == (row & 127)))
            lats.append(subs((128, 128)) == (row >> 7))
        hot = jnp.concatenate(hots, axis=1)
        hit = dot_nn(left, jnp.concatenate([hot, hot, hot], axis=0))
        for f in range(fields):
            for i in range(2):
                part = hit[128 * f : 128 * (f + 1), 128 * i : 128 * (i + 1)]
                hold[pl.ds(8 * f + 2 * pair + i, 1), :] = jnp.sum(
                    jnp.where(lats[i], part, 0.0), axis=0, keepdims=True
                )
    rows = hold[...]
    for z in range(found.shape[0] // rows.shape[0]):
        found[pl.ds(z * rows.shape[0], rows.shape[0]), :] = rows


def scatter(levels, tab, pulled, east, west, columns):
    fields = pulled.shape[0]
    rows = 8 * fields
    here = lax.axis_index("obs")
    top = levels.shape[0] // rows - 1

    def level(k):
        return levels[pl.ds(pl.multiple_of(jnp.clip(k, 0, top) * rows, rows), rows), :]

    own, above, below = level(here), level(here + 1), level(here - 1)
    d, o, u, b = (tab[pl.ds(rows * k, rows), :] for k in range(4))
    amount = d * own + o * above + u * below - b
    cells = tab[pl.ds(4 * rows, 8), :].astype(I32)
    lat = [subs((128, 128)) == (cells[s : s + 1] >> 7) for s in range(8)]
    hot = jnp.concatenate(
        [one_hot(subs((128, 128)) == (cells[s : s + 1] & 127)) for s in range(8)], axis=1
    )
    for f in range(fields):
        total = jnp.zeros((128, 128), F32)
        for part in split3(amount[8 * f : 8 * f + 8]):
            wide = part.astype(F32)
            left = jnp.concatenate(
                [jnp.where(lat[s], wide[s : s + 1], 0.0).astype(BF16) for s in range(8)], axis=1
            )
            total = total + dot_nt(left, hot)
        pulled[f] = total
    pack_edges([pulled[f] for f in range(fields)], east, west)
    for half in range(2):
        turned_block = levels[pl.ds(128 * half, 128), :].T
        for k in range(2):
            columns[:, 2 * k + half, :] = turned_block[64 * k : 64 * (k + 1)]


def depart(columns, holder, slots, prof, field, level, weight, innov, prec, out):
    profiles = holder.shape[1]
    left = jnp.concatenate(
        [
            jnp.concatenate([columns[:, half, :], columns[:, 2 + half, :]], axis=0).T
            for half in range(2)
        ],
        axis=0,
    )
    place = slots[...].astype(I32)
    row = subs((128, profiles))
    held = one_hot(((row & 63) == holder[...]) & ((row >> 6) == (place & 1)))
    spread = dot_nn(
        jnp.concatenate(split3(left), axis=1), jnp.concatenate([held, held, held], axis=0)
    )
    mine = subs((8, profiles)) == (place >> 1)
    values = jnp.concatenate(
        [
            jnp.sum(jnp.where(mine, spread[8 * r : 8 * r + 8], 0.0), axis=0, keepdims=True)
            for r in range(32)
        ],
        axis=0,
    )
    hot = jnp.concatenate(
        [one_hot(subs((profiles, 128)) == prof[pl.ds(c, 1), :]) for c in range(4)], axis=1
    )
    seen = sum(dot_nn(part, hot) for part in split3(values))
    row = subs((32, 128))
    for c in range(4):
        at = pl.ds(c, 1)
        code = level[at, :] * 4 + field[at, :]
        part = seen[:, 128 * c : 128 * (c + 1)]
        low = jnp.sum(jnp.where(row == code, part, 0.0), axis=0, keepdims=True)
        high = jnp.sum(jnp.where(row == code + 4, part, 0.0), axis=0, keepdims=True)
        w = weight[at, :]
        out[at, :] = prec[at, :] * (w * low + (1.0 - w) * high - innov[at, :])


def ring(axis, by):
    count = lax.axis_size(axis)
    return [(i, (i + by) % count) for i in range(count)]


def pair(forward, back, axis):
    return (
        lax.ppermute(forward, axis, ring(axis, 1)),
        lax.ppermute(back, axis, ring(axis, -1)),
    )


def exchange(x, axes):
    return lax.all_to_all(x, axes, 0, 0, tiled=True)


def assimilate(
    control,
    diffusivity,
    prof_tile,
    prof_cell,
    obs_prof,
    obs_field,
    obs_level,
    obs_weight,
    innovation,
    obs_precision,
):
    fields, _, ny, nx = control.shape
    tile = (ny, nx)
    profiles = prof_tile.shape[0]
    holders = lax.axis_size("gx") * lax.axis_size("gy")
    levels = lax.axis_size("obs")
    ext = ny + 2 * ROWS
    ctl = control.reshape(fields, ny, nx)
    rate = diffusivity.reshape(2, ny, nx)
    holder = prof_tile.reshape(1, profiles)
    cell = prof_cell.reshape(1, profiles)
    obs = [
        x.reshape(4, 128)
        for x in (obs_prof, obs_field, obs_level, obs_weight, innovation, obs_precision)
    ]
    planes = pltpu.VMEM((2 * fields, ext + 2 * PAD, nx), F32)

    given = [pltpu.with_memory_space_constraint(x, pltpu.HBM) for x in (ctl, rate, holder, cell, *obs)]
    east, west, rows, ctl, rate, holder, cell, *obs = call(
        pack_inputs,
        [tile, tile, (levels * 16, 128)] + [jax.ShapeDtypeStruct(x.shape, x.dtype) for x in given],
        given,
        [pltpu.SemaphoreType.DMA((len(given),))],
        hbm=True,
    )
    left, right = pair(east, west, "gx")
    rows = exchange(rows, "obs")
    side = (fields + 3, ROWS, nx)
    strip, north, south = call(edges_first, [tile, side, side], [ctl, rate, left, right])
    south, north = pair(north, south, "gy")
    table, slots = call(
        tables, [(holders, 3, 128), (1, profiles)], [rows, holder, cell], flops=400_000_000
    )
    table = exchange(table, ("gx", "gy"))
    inc, coef = call(
        diffuse_control,
        [(fields, ny, nx), (10, ext, nx)],
        [ctl, rate, strip, south, north],
        [planes, planes, pltpu.VMEM((4, ext + 2 * PAD, nx), F32)],
        flops=40_000_000,
    )
    found, tab = call(
        gather,
        [(levels * fields * 8, 128), (136, 128)],
        [inc, table],
        [pltpu.VMEM((fields * 8, 128), F32)],
        flops=400_000_000,
    )
    found = exchange(found, "obs")
    pulled, east, west, columns = call(
        scatter,
        [(fields, ny, nx), tile, tile, (holders, 4, 128)],
        [found, tab],
        flops=400_000_000,
    )
    left, right = pair(east, west, "gx")
    columns = exchange(columns, ("gx", "gy"))
    side = (fields + 1, ROWS, nx)
    strip, north, south = call(edges_second, [tile, side, side], [pulled, left, right])
    south, north = pair(north, south, "gy")
    (gradient,) = call(
        diffuse_pulled,
        [(fields, ny, nx)],
        [pulled, strip, south, north, coef, ctl],
        [planes, planes],
        flops=40_000_000,
    )
    (departures,) = call(depart, [(4, 128)], [columns, holder, slots, *obs], flops=400_000_000)
    return gradient.reshape(control.shape), departures.reshape(obs_prof.shape)


def solution(mesh):
    in_specs = (
        P(None, "obs", "gy", "gx"),
        P(None, "obs", "gy", "gx"),
        P(("gx", "gy"), None),
        P(("gx", "gy")),
        P(("gx", "gy", "obs")),
        P(("gx", "gy", "obs")),
        P(("gx", "gy", "obs")),
        P(("gx", "gy", "obs")),
        P(("gx", "gy", "obs")),
        P(("gx", "gy", "obs")),
    )
    out_specs = (P(None, "obs", "gy", "gx"), P(("gx", "gy", "obs")))
    return jax.shard_map(
        assimilate, mesh=mesh, in_specs=in_specs, out_specs=out_specs, check_vma=False
    )
```

```python
import jax
import jax.numpy as jnp
from jax import lax
from jax.experimental import pallas as pl
from jax.experimental.pallas import tpu as pltpu
from jax.sharding import PartitionSpec as P


STEPS = 10
HALO = STEPS
ROWS = 16
PITCH = 2 * HALO
PAD = 8
F32, BF16, I32 = jnp.float32, jnp.bfloat16, jnp.int32


def lanes(shape):
    return lax.broadcasted_iota(I32, shape, len(shape) - 1)


def subs(shape):
    return lax.broadcasted_iota(I32, shape, len(shape) - 2)


def split3(x):
    hi = x.astype(BF16)
    rest = x - hi.astype(F32)
    mid = rest.astype(BF16)
    low = (rest - mid.astype(F32)).astype(BF16)
    return hi, mid, low


def one_hot(flags):
    return jnp.where(flags, 1.0, 0.0).astype(BF16)


def dot_nn(a, b):
    return lax.dot_general(a, b, (((1,), (0,)), ((), ())), preferred_element_type=F32)


def dot_nt(a, b):
    return lax.dot_general(a, b, (((1,), (1,)), ((), ())), preferred_element_type=F32)


def call(body, outs, args, scratch=(), flops=1_000_000, hbm=False):
    vmem = pl.BlockSpec(memory_space=pltpu.VMEM)
    given = pl.BlockSpec(memory_space=pltpu.HBM) if hbm else vmem
    outs = [o if isinstance(o, jax.ShapeDtypeStruct) else jax.ShapeDtypeStruct(o, F32) for o in outs]
    return pl.pallas_call(
        body,
        out_shape=outs,
        in_specs=[given] * len(args),
        out_specs=[vmem] * len(outs),
        scratch_shapes=list(scratch),
        cost_estimate=pl.CostEstimate(
            flops=flops,
            bytes_accessed=sum(4 * x.size for x in (*args, *outs)),
            transcendentals=0,
        ),
        compiler_params=pltpu.CompilerParams(vmem_limit_bytes=16 << 20),
    )(*args)


def mask_north(rate_ref):
    last = rate_ref.shape[1] - 8
    rows = rate_ref[1, pl.ds(last, 8), :]
    top = lax.axis_index("gy") == lax.axis_size("gy") - 1
    rate_ref[1, pl.ds(last, 8), :] = jnp.where(top & (subs(rows.shape) == 7), 0.0, rows)


def pack_edges(arrays, east_ref, west_ref):
    lane = lanes(arrays[0].shape)
    east = jnp.zeros(arrays[0].shape, F32)
    west = jnp.zeros(arrays[0].shape, F32)
    for a, x in enumerate(arrays):
        width = x.shape[-1]
        low = a * PITCH + HALO
        moved = pltpu.roll(x, (low - (width - HALO)) % width, 1)
        east = jnp.where((lane >= low) & (lane < low + HALO), moved, east)
        low = a * PITCH
        moved = pltpu.roll(x, low % width, 1) if low else x
        west = jnp.where((lane >= low) & (lane < low + HALO), moved, west)
    east_ref[...] = east
    west_ref[...] = west


def pack_inputs(*refs):
    sources, (east, west, obs), kept, sems = refs[:10], refs[10:13], refs[13:23], refs[23]
    copies = [
        pltpu.make_async_copy(source, target, sems.at[i])
        for i, (source, target) in enumerate(zip(sources, kept))
    ]
    for copy in copies:
        copy.start()
    for copy in copies:
        copy.wait()
    ctl, rate, _, _, prof, field, level, weight, innov, prec = kept
    mask_north(rate)
    pack_edges([ctl[f] for f in range(ctl.shape[0])] + [rate[0], rate[1]], east, west)
    index = ((field[...] * 8 + level[...]) * 512 + prof[...]).astype(F32)
    rows = jnp.concatenate([index, weight[...], innov[...], prec[...]], axis=0)
    for z in range(obs.shape[0] // rows.shape[0]):
        obs[pl.ds(z * rows.shape[0], rows.shape[0]), :] = rows


def odd():
    return lax.rem(lax.axis_index("gy"), 2)


def pick(first, second):
    return pl.multiple_of(jnp.where(odd() == 0, first, second), 8)


def meet(refs, strip, first, second):
    last = strip.shape[0] - ROWS
    for target, at in ((first, pick(last, 0)), (second, pick(0, last))):
        for a, ref in enumerate(refs + [strip]):
            target[a] = ref[pl.ds(at, ROWS), :]


def edges_first(ctl, rate, left, right, strip, first, second):
    strip[...] = left[...] + right[...]
    refs = [ctl.at[f] for f in range(ctl.shape[0])] + [rate.at[0], rate.at[1]]
    meet(refs, strip, first, second)


def edges_second(pulled, left, right, strip, first, second):
    strip[...] = left[...] + right[...]
    meet([pulled.at[f] for f in range(pulled.shape[0])], strip, first, second)


def unpack(block, a):
    width = block.shape[-1]
    east = pltpu.roll(block, (-a * PITCH) % width, 1) if a else block
    west = pltpu.roll(block, (width - HALO - a * PITCH - HALO) % width, 1)
    return jnp.where(lanes(block.shape) < width // 2, east, west)


def blocks(own, first, second):
    low, high = PAD, PAD + ROWS + own.shape[0]
    return ((pick(high, low), first), (PAD + ROWS, own), (pick(low, high), second))


def turned(main, beyond, by):
    width = main.shape[-1]
    edge = lanes(main.shape) == (0 if by == 1 else width - 1)
    a = pltpu.roll(main, by % width, 1)
    b = pltpu.roll(beyond, by % width, 1)
    return jnp.where(edge, b, a), jnp.where(edge, a, b)


def one_step(source, coef, store, first, last):
    fields = source.shape[0] // 2
    for tile in range(first, last):
        row = PAD + 8 * tile
        here, up, down = pl.ds(row, 8), pl.ds(row + 1, 8), pl.ds(row - 1, 8)
        c = [coef[i, pl.ds(8 * tile, 8), :] for i in range(10)]
        for f in range(fields):
            m, s = source[2 * f, here, :], source[2 * f + 1, here, :]
            me, se = turned(m, s, -1)
            mw, sw = turned(m, s, 1)
            new_m = c[0] * m + c[2] * me + c[4] * mw + c[6] * source[2 * f, up, :]
            new_m = new_m + c[8] * source[2 * f, down, :]
            new_s = c[1] * s + c[3] * se + c[5] * sw + c[7] * source[2 * f + 1, up, :]
            new_s = new_s + c[9] * source[2 * f + 1, down, :]
            store(f, tile, new_m, new_s)


def ten_steps(a, b, coef, finish, tiles):
    def into(target):
        def store(f, tile, main, beyond):
            target[2 * f, pl.ds(PAD + 8 * tile, 8), :] = main
            target[2 * f + 1, pl.ds(PAD + 8 * tile, 8), :] = beyond

        return store

    one_step(a, coef, into(b), 0, tiles)

    def body(_, carry):
        one_step(b, coef, into(a), 1, tiles - 1)
        one_step(a, coef, into(b), 1, tiles - 1)
        return carry

    lax.fori_loop(0, STEPS // 2 - 1, body, 0)

    def store(f, tile, main, beyond):
        finish(f, 8 * tile - ROWS, main)

    one_step(b, coef, store, ROWS // 8, tiles - ROWS // 8)


def load_field(a, own, strip, first, second, packed):
    fields = own.shape[0]
    for f in range(fields):
        for row, block in blocks(own[f], first[f], second[f]):
            a[2 * f, pl.ds(row, block.shape[0]), :] = block
    for row, block in blocks(strip[...], first[packed], second[packed]):
        for f in range(fields):
            a[2 * f + 1, pl.ds(row, block.shape[0]), :] = unpack(block, f)
    clear = jnp.zeros((PAD, a.shape[2]), F32)
    for plane in range(a.shape[0]):
        a[plane, pl.ds(0, PAD), :] = clear
        a[plane, pl.ds(a.shape[1] - PAD, PAD), :] = clear


def diffuse_control(ctl, rate, strip, first, second, inc, coef, a, b, rates):
    fields = ctl.shape[0]
    tiles = coef.shape[1] // 8
    own_rates = (rate[0], rate[1])
    for k in range(2):
        for row, block in blocks(own_rates[k], first[fields + k], second[fields + k]):
            rates[2 * k, pl.ds(row, block.shape[0]), :] = block
        for row, block in blocks(strip[...], first[fields + 2], second[fields + 2]):
            lane = lanes(block.shape)
            near = (lane < HALO) | (lane >= block.shape[-1] - HALO)
            rates[2 * k + 1, pl.ds(row, block.shape[0]), :] = jnp.where(
                near, unpack(block, fields + k), 0.0
            )
        clear = jnp.zeros((PAD, rates.shape[2]), F32)
        for plane in (2 * k, 2 * k + 1):
            rates[plane, pl.ds(0, PAD), :] = clear
    for tile in range(tiles):
        here, down = pl.ds(PAD + 8 * tile, 8), pl.ds(PAD + 8 * tile - 1, 8)
        east = (rates[0, here, :], rates[1, here, :])
        west = turned(east[0], east[1], 1)
        for plane in range(2):
            n, s = rates[2 + plane, here, :], rates[2 + plane, down, :]
            e, w = east[plane], west[plane]
            for i, value in enumerate((1.0 - e - w - n - s, e, w, n, s)):
                coef[2 * i + plane, pl.ds(8 * tile, 8), :] = value
    load_field(a, ctl, strip, first, second, fields + 2)

    def finish(f, row, main):
        inc[f, pl.ds(row, 8), :] = main

    ten_steps(a, b, coef, finish, tiles)


def diffuse_pulled(pulled, strip, first, second, coef, ctl, grad, a, b):
    load_field(a, pulled, strip, first, second, pulled.shape[0])

    def finish(f, row, main):
        grad[f, pl.ds(row, 8), :] = ctl[f, pl.ds(row, 8), :] + main

    ten_steps(a, b, coef, finish, coef.shape[1] // 8)


def tables(obs, holder, cell, out, slots):
    profiles = holder.shape[1]
    level_here = lax.axis_index("obs")
    groups = obs.shape[0] // 16
    width = obs.shape[1]
    acc = jnp.zeros((48, profiles), F32)
    row16 = subs((16, width))
    for z in range(groups):
        parts = ([], [], [])
        hots = []
        for c in range(4):
            at = 16 * z + c
            index = obs[pl.ds(at, 1), :].astype(I32)
            w, y, q = (obs[pl.ds(at + 4 * k, 1), :] for k in (1, 2, 3))
            prof = index & 511
            level = (index >> 9) & 7
            field = index >> 12
            low = jnp.where(level == level_here, q, 0.0)
            high = jnp.where(level == level_here - 1, q, 0.0)
            v = 1.0 - w
            lw, hv = low * w, high * v
            rows = (lw * w + hv * v, lw * v, hv * w, (lw + hv) * y)
            value = jnp.where(
                row16 < 8,
                jnp.where(row16 < 4, rows[0], rows[1]),
                jnp.where(row16 < 12, rows[2], rows[3]),
            )
            value = jnp.where((row16 & 3) == field, value, 0.0)
            for part, x in zip(parts, split3(value)):
                part.append(x)
            hots.append(one_hot(subs((profiles, width)) == prof))
        left = jnp.concatenate([jnp.concatenate(p, axis=1) for p in parts], axis=0)
        acc = acc + dot_nt(left, jnp.concatenate(hots, axis=1))
    table = acc[0:16] + acc[16:32] + acc[32:48]
    held = subs((out.shape[0], profiles)) == holder[...]
    held16 = one_hot(held)
    before = one_hot(subs((profiles, profiles)) < lanes((profiles, profiles)))
    slot = jnp.sum(jnp.where(held, dot_nn(held16, before), 0.0), axis=0, keepdims=True)
    slots[...] = slot
    place = slot.astype(I32)
    cells = cell[...].astype(F32)
    mine = [subs((8, profiles)) * 2 + k == place for k in range(2)]
    for k in range(2):
        value = jnp.concatenate(
            [jnp.where(mine[k], table[r : r + 1], 0.0) for r in range(16)], axis=0
        )
        total = sum(dot_nt(held16, part) for part in split3(value))
        out[:, 0, pl.ds(128 * k, 128)] = total
    value = jnp.concatenate(
        [jnp.where(mine[k], cells, 0.0) for k in range(2)]
        + [jnp.zeros((112, profiles), F32)],
        axis=0,
    )
    out[:, 0, pl.ds(256, 128)] = sum(dot_nt(held16, part) for part in split3(value)[:2])


def gather(inc, sent, found, tab, hold):
    fields = inc.shape[0]
    tab[pl.ds(0, 128), :] = jnp.concatenate([sent[:, 0, pl.ds(0, 128)], sent[:, 0, pl.ds(128, 128)]], axis=0).T
    cells = sent[:, 0, pl.ds(256, 128)]
    cells = jnp.concatenate([cells, cells], axis=0).T
    cells = jnp.where(lanes((8, 128)) < 64, cells[0:8], cells[8:16])
    tab[pl.ds(128, 8), :] = cells
    cells = cells.astype(I32)
    left = jnp.concatenate(
        [jnp.concatenate(split3(inc[f]), axis=1) for f in range(fields)], axis=0
    )
    for pair in range(4):
        hots, lats = [], []
        for s in (2 * pair, 2 * pair + 1):
            row = cells[s : s + 1]
            hots.append(one_hot(subs((128, 128)) == (row & 127)))
            lats.append(subs((128, 128)) == (row >> 7))
        hot = jnp.concatenate(hots, axis=1)
        hit = dot_nn(left, jnp.concatenate([hot, hot, hot], axis=0))
        for f in range(fields):
            for i in range(2):
                part = hit[128 * f : 128 * (f + 1), 128 * i : 128 * (i + 1)]
                hold[pl.ds(8 * f + 2 * pair + i, 1), :] = jnp.sum(
                    jnp.where(lats[i], part, 0.0), axis=0, keepdims=True
                )
    rows = hold[...]
    for z in range(found.shape[0] // rows.shape[0]):
        found[pl.ds(z * rows.shape[0], rows.shape[0]), :] = rows


def scatter(levels, tab, pulled, east, west, columns):
    fields = pulled.shape[0]
    rows = 8 * fields
    here = lax.axis_index("obs")
    top = levels.shape[0] // rows - 1

    def level(k):
        return levels[pl.ds(pl.multiple_of(jnp.clip(k, 0, top) * rows, rows), rows), :]

    own, above, below = level(here), level(here + 1), level(here - 1)
    d, o, u, b = (tab[pl.ds(rows * k, rows), :] for k in range(4))
    amount = d * own + o * above + u * below - b
    cells = tab[pl.ds(4 * rows, 8), :].astype(I32)
    lat = [subs((128, 128)) == (cells[s : s + 1] >> 7) for s in range(8)]
    hot = jnp.concatenate(
        [one_hot(subs((128, 128)) == (cells[s : s + 1] & 127)) for s in range(8)], axis=1
    )
    for f in range(fields):
        total = jnp.zeros((128, 128), F32)
        for part in split3(amount[8 * f : 8 * f + 8]):
            wide = part.astype(F32)
            left = jnp.concatenate(
                [jnp.where(lat[s], wide[s : s + 1], 0.0).astype(BF16) for s in range(8)], axis=1
            )
            total = total + dot_nt(left, hot)
        pulled[f] = total
    pack_edges([pulled[f] for f in range(fields)], east, west)
    for half in range(2):
        turned_block = levels[pl.ds(128 * half, 128), :].T
        for k in range(2):
            columns[:, 2 * k + half, :] = turned_block[64 * k : 64 * (k + 1)]


def depart(columns, holder, slots, prof, field, level, weight, innov, prec, out):
    profiles = holder.shape[1]
    left = jnp.concatenate(
        [
            jnp.concatenate([columns[:, half, :], columns[:, 2 + half, :]], axis=0).T
            for half in range(2)
        ],
        axis=0,
    )
    place = slots[...].astype(I32)
    row = subs((128, profiles))
    held = one_hot(((row & 63) == holder[...]) & ((row >> 6) == (place & 1)))
    spread = dot_nn(
        jnp.concatenate(split3(left), axis=1), jnp.concatenate([held, held, held], axis=0)
    )
    mine = subs((8, profiles)) == (place >> 1)
    values = jnp.concatenate(
        [
            jnp.sum(jnp.where(mine, spread[8 * r : 8 * r + 8], 0.0), axis=0, keepdims=True)
            for r in range(32)
        ],
        axis=0,
    )
    hot = jnp.concatenate(
        [one_hot(subs((profiles, 128)) == prof[pl.ds(c, 1), :]) for c in range(4)], axis=1
    )
    seen = sum(dot_nn(part, hot) for part in split3(values))
    row = subs((32, 128))
    for c in range(4):
        at = pl.ds(c, 1)
        code = level[at, :] * 4 + field[at, :]
        part = seen[:, 128 * c : 128 * (c + 1)]
        low = jnp.sum(jnp.where(row == code, part, 0.0), axis=0, keepdims=True)
        high = jnp.sum(jnp.where(row == code + 4, part, 0.0), axis=0, keepdims=True)
        w = weight[at, :]
        out[at, :] = prec[at, :] * (w * low + (1.0 - w) * high - innov[at, :])


def ring(axis, by):
    count = lax.axis_size(axis)
    return [(i, (i + by) % count) for i in range(count)]


def pair(forward, back, axis):
    return (
        lax.ppermute(forward, axis, ring(axis, 1)),
        lax.ppermute(back, axis, ring(axis, -1)),
    )


def swap(first, second, axis):
    count = lax.axis_size(axis)
    low = [(i, i ^ 1) for i in range(count)]
    high = [(i, (i + 1 ^ 1) - 1) for i in range(1, count - 1)]
    return lax.ppermute(first, axis, low), lax.ppermute(second, axis, high)


def exchange(x, axes):
    return lax.all_to_all(x, axes, 0, 0, tiled=True)


def assimilate(
    control,
    diffusivity,
    prof_tile,
    prof_cell,
    obs_prof,
    obs_field,
    obs_level,
    obs_weight,
    innovation,
    obs_precision,
):
    fields, _, ny, nx = control.shape
    tile = (ny, nx)
    profiles = prof_tile.shape[0]
    holders = lax.axis_size("gx") * lax.axis_size("gy")
    levels = lax.axis_size("obs")
    ext = ny + 2 * ROWS
    ctl = control.reshape(fields, ny, nx)
    rate = diffusivity.reshape(2, ny, nx)
    holder = prof_tile.reshape(1, profiles)
    cell = prof_cell.reshape(1, profiles)
    obs = [
        x.reshape(4, 128)
        for x in (obs_prof, obs_field, obs_level, obs_weight, innovation, obs_precision)
    ]
    planes = pltpu.VMEM((2 * fields, ext + 2 * PAD, nx), F32)

    given = [pltpu.with_memory_space_constraint(x, pltpu.HBM) for x in (ctl, rate, holder, cell, *obs)]
    east, west, rows, ctl, rate, holder, cell, *obs = call(
        pack_inputs,
        [tile, tile, (levels * 16, 128)] + [jax.ShapeDtypeStruct(x.shape, x.dtype) for x in given],
        given,
        [pltpu.SemaphoreType.DMA((len(given),))],
        hbm=True,
    )
    left, right = pair(east, west, "gx")
    rows = exchange(rows, "obs")
    side = (fields + 3, ROWS, nx)
    strip, first, second = call(edges_first, [tile, side, side], [ctl, rate, left, right])
    first, second = swap(first, second, "gy")
    table, slots = call(
        tables, [(holders, 1, 384), (1, profiles)], [rows, holder, cell], flops=400_000_000
    )
    table = exchange(table, ("gx", "gy"))
    inc, coef = call(
        diffuse_control,
        [(fields, ny, nx), (10, ext, nx)],
        [ctl, rate, strip, first, second],
        [planes, planes, pltpu.VMEM((4, ext + 2 * PAD, nx), F32)],
        flops=40_000_000,
    )
    found, tab = call(
        gather,
        [(levels * fields * 8, 128), (136, 128)],
        [inc, table],
        [pltpu.VMEM((fields * 8, 128), F32)],
        flops=400_000_000,
    )
    found = exchange(found, "obs")
    pulled, east, west, columns = call(
        scatter,
        [(fields, ny, nx), tile, tile, (holders, 4, 128)],
        [found, tab],
        flops=400_000_000,
    )
    left, right = pair(east, west, "gx")
    columns = exchange(columns, ("gx", "gy"))
    side = (fields + 1, ROWS, nx)
    strip, first, second = call(edges_second, [tile, side, side], [pulled, left, right])
    first, second = swap(first, second, "gy")
    (gradient,) = call(
        diffuse_pulled,
        [(fields, ny, nx)],
        [pulled, strip, first, second, coef, ctl],
        [planes, planes],
        flops=40_000_000,
    )
    (departures,) = call(depart, [(4, 128)], [columns, holder, slots, *obs], flops=400_000_000)
    return gradient.reshape(control.shape), departures.reshape(obs_prof.shape)


def solution(mesh):
    in_specs = (
        P(None, "obs", "gy", "gx"),
        P(None, "obs", "gy", "gx"),
        P(("gx", "gy"), None),
        P(("gx", "gy")),
        P(("gx", "gy", "obs")),
        P(("gx", "gy", "obs")),
        P(("gx", "gy", "obs")),
        P(("gx", "gy", "obs")),
        P(("gx", "gy", "obs")),
        P(("gx", "gy", "obs")),
    )
    out_specs = (P(None, "obs", "gy", "gx"), P(("gx", "gy", "obs")))
    return jax.shard_map(
        assimilate, mesh=mesh, in_specs=in_specs, out_specs=out_specs, check_vma=False
    )
```

```python
import jax
import jax.numpy as jnp
from jax import lax
from jax.experimental import pallas as pl
from jax.experimental.pallas import tpu as pltpu
from jax.sharding import PartitionSpec as P


STEPS = 10
HALO = STEPS
ROWS = 16
EAST_AT, NORTH_AT = HALO, 74
PAD = 8
F32, BF16, I32 = jnp.float32, jnp.bfloat16, jnp.int32


def lanes(shape):
    return lax.broadcasted_iota(I32, shape, len(shape) - 1)


def subs(shape):
    return lax.broadcasted_iota(I32, shape, len(shape) - 2)


def split3(x):
    hi = x.astype(BF16)
    rest = x - hi.astype(F32)
    mid = rest.astype(BF16)
    low = (rest - mid.astype(F32)).astype(BF16)
    return hi, mid, low


def one_hot(flags):
    return jnp.where(flags, 1.0, 0.0).astype(BF16)


def dot_nn(a, b):
    return lax.dot_general(a, b, (((1,), (0,)), ((), ())), preferred_element_type=F32)


def dot_nt(a, b):
    return lax.dot_general(a, b, (((1,), (1,)), ((), ())), preferred_element_type=F32)


def call(body, outs, args, scratch=(), flops=1_000_000, hbm=False):
    vmem = pl.BlockSpec(memory_space=pltpu.VMEM)
    given = pl.BlockSpec(memory_space=pltpu.HBM) if hbm else vmem
    outs = [o if isinstance(o, jax.ShapeDtypeStruct) else jax.ShapeDtypeStruct(o, F32) for o in outs]
    return pl.pallas_call(
        body,
        out_shape=outs,
        in_specs=[given] * len(args),
        out_specs=[vmem] * len(outs),
        scratch_shapes=list(scratch),
        cost_estimate=pl.CostEstimate(
            flops=flops,
            bytes_accessed=sum(4 * x.size for x in (*args, *outs)),
            transcendentals=0,
        ),
        compiler_params=pltpu.CompilerParams(vmem_limit_bytes=16 << 20),
    )(*args)


def mask_north(rate_ref):
    last = rate_ref.shape[1] - 8
    rows = rate_ref[1, pl.ds(last, 8), :]
    top = lax.axis_index("gy") == lax.axis_size("gy") - 1
    rate_ref[1, pl.ds(last, 8), :] = jnp.where(top & (subs(rows.shape) == 7), 0.0, rows)


def offset(f, planes, width):
    return f * (width // planes)


def turn(x, by):
    by %= x.shape[-1]
    return pltpu.roll(x, by, x.ndim - 1) if by else x


def within(shape, low):
    width = shape[-1]
    return ((lanes(shape) - low % width + width) & (width - 1)) < HALO


def pack_edges(turned, rates, east_ref, west_ref):
    shape = turned[0].shape
    width = shape[-1]
    east = west = jnp.zeros(shape, F32)
    for f, x in enumerate(turned):
        low = offset(f, len(turned), width)
        east = jnp.where(within(shape, low - HALO), x, east)
        west = jnp.where(within(shape, low), x, west)
    for at, x in rates:
        east = jnp.where(within(shape, at), turn(x, at + HALO - width), east)
        west = jnp.where(within(shape, at + 32), turn(x, at + 32), west)
    east_ref[...] = east
    west_ref[...] = west


def pack_inputs(*refs):
    sources, (east, west, obs, turned), kept, (ctl, sems) = refs[:10], refs[10:14], refs[14:23], refs[23:]
    copies = [
        pltpu.make_async_copy(source, target, sems.at[i])
        for i, (source, target) in enumerate(zip(sources, (ctl, *kept)))
    ]
    for copy in copies:
        copy.start()
    for copy in copies:
        copy.wait()
    rate, _, _, prof, field, level, weight, innov, prec = kept
    mask_north(rate)
    fields = ctl.shape[0]
    planes = [turn(ctl[f], offset(f, fields, ctl.shape[2])) for f in range(fields)]
    for f in range(fields):
        turned[f] = planes[f]
    pack_edges(planes, ((EAST_AT, rate[0]), (NORTH_AT, rate[1])), east, west)
    index = ((field[...] * 8 + level[...]) * 512 + prof[...]).astype(F32)
    rows = jnp.concatenate([index, weight[...], innov[...], prec[...]], axis=0)
    for z in range(obs.shape[0] // rows.shape[0]):
        obs[pl.ds(z * rows.shape[0], rows.shape[0]), :] = rows


def odd():
    return lax.rem(lax.axis_index("gy"), 2)


def pick(first, second):
    return pl.multiple_of(jnp.where(odd() == 0, first, second), 8)


def meet(refs, strip, first, second):
    last = strip.shape[0] - ROWS
    for target, at in ((first, pick(last, 0)), (second, pick(0, last))):
        for a, ref in enumerate(refs + [strip]):
            target[a] = ref[pl.ds(at, ROWS), :]


def edges_first(own, rate, left, right, strip, first, second):
    strip[...] = left[...] + right[...]
    refs = [own.at[f] for f in range(own.shape[0])] + [rate.at[0], rate.at[1]]
    meet(refs, strip, first, second)


def edges_second(pulled, left, right, strip, first, second):
    strip[...] = left[...] + right[...]
    meet([pulled.at[f] for f in range(pulled.shape[0])], strip, first, second)


def blocks(own, first, second):
    low, high = PAD, PAD + ROWS + own.shape[0]
    return ((pick(high, low), first), (PAD + ROWS, own), (pick(low, high), second))


def one_step(source, target, coef):
    fields = source.shape[0] - 1
    width = source.shape[2]
    for tile in range(coef.shape[0]):
        row = PAD + 8 * tile
        here, up, down = pl.ds(row, 8), pl.ds(row + 1, 8), pl.ds(row - 1, 8)
        lane = lanes((8, width))

        def new(p, v, east, west):
            c = [coef[tile, 5 * p + i] for i in range(5)]
            total = c[0] * v + c[1] * east + c[2] * west
            target[p, here, :] = total + c[3] * source[p, up, :] + c[4] * source[p, down, :]

        strip = source[fields, here, :]
        strip_east = next_east = turn(strip, -1)
        strip_west = next_west = turn(strip, 1)
        for f in range(fields):
            v = source[f, here, :]
            start = lane == offset(f, fields, width)
            stop = lane == (offset(f, fields, width) - 1) % width
            east, west = turn(v, -1), turn(v, 1)
            next_east = jnp.where(stop, east, next_east)
            next_west = jnp.where(start, west, next_west)
            new(f, v, jnp.where(stop, strip_east, east), jnp.where(start, strip_west, west))
        new(fields, strip, next_east, next_west)


def ten_steps(a, b, coef):
    def body(_):
        one_step(a, b, coef)
        one_step(b, a, coef)

    each(STEPS // 2, body)


def each(count, body):
    def step(i, carry):
        body(i)
        return carry

    lax.fori_loop(0, count, step, 0)


def rows_at(start, size):
    return pl.ds(pl.multiple_of(start, 8), size)


def clear_ends(a):
    clear = jnp.zeros((PAD, a.shape[2]), F32)
    for plane in range(a.shape[0]):
        a[plane, pl.ds(0, PAD), :] = clear
        a[plane, pl.ds(a.shape[1] - PAD, PAD), :] = clear


def load_field(a, b, own, strip, first, second, packed):
    fields = own.shape[0]
    for f in range(fields):
        for row, block in blocks(own[f], first[f], second[f]):
            a[f, pl.ds(row, block.shape[0]), :] = block
    for row, block in blocks(strip[...], first[packed], second[packed]):
        a[fields, pl.ds(row, block.shape[0]), :] = block
    clear_ends(a)
    clear_ends(b)


def rate_strip(packed, at, fields):
    shape = packed.shape
    width = shape[-1]
    east = turn(packed, -at - 32)
    west = turn(packed, width - HALO - at)
    g = jnp.where(within(shape, 0), east, jnp.where(within(shape, -HALO), west, 0.0))
    by = width // fields
    while by < width:
        g = g + turn(g, by)
        by *= 2
    return g


def diffuse_control(own, rate, strip, first, second, inc, coef, a, b, wide, north):
    fields, height, width = own.shape
    load_field(a, b, own, strip, first, second, fields + 2)
    for k in range(2):
        for row, block in blocks(rate[k], first[fields + k], second[fields + k]):
            wide[k, pl.ds(row, block.shape[0]), :] = block
    north[:, pl.ds(0, PAD), :] = jnp.zeros((fields + 1, PAD, width), F32)
    size = 80

    def turned(block):
        here = rows_at(PAD + size * block, size)
        n = wide[1, here, :]
        for f in range(fields):
            north[f, here, :] = turn(n, offset(f, fields, width))
        north[fields, here, :] = rate_strip(a[fields, here, :], NORTH_AT, fields)
        for k in range(size // 8):
            tile = size // 8 * block + k
            e = wide[0, rows_at(PAD + 8 * tile, 8), :]
            beyond = rate_strip(a[fields, rows_at(PAD + 8 * tile, 8), :], EAST_AT, fields)
            before = strip_before = turn(beyond, 1)
            lane = lanes((8, width))
            planes = []
            for f in range(fields):
                low = offset(f, fields, width)
                start = lane == low
                moved = turn(e, low + 1)
                strip_before = jnp.where(start, moved, strip_before)
                planes.append((turn(e, low), jnp.where(start, before, moved)))
            planes.append((beyond, strip_before))
            for p, (east, west) in enumerate(planes):
                both = north[p, rows_at(8 * tile, 16), :]
                n, s = both[8:], both[7:15]
                for i, value in enumerate((1.0 - east - west - n - s, east, west, n, s)):
                    coef[tile, 5 * p + i] = value

    each(coef.shape[0] * 8 // size, turned)
    ten_steps(a, b, coef)
    size = 64

    def back(block):
        for f in range(fields):
            value = a[f, rows_at(PAD + ROWS + size * block, size), :]
            inc[f, rows_at(size * block, size), :] = turn(value, -offset(f, fields, width))

    each(height // size, back)


def diffuse_pulled(pulled, strip, first, second, coef, own, grad, a, b):
    fields, height, width = pulled.shape
    load_field(a, b, pulled, strip, first, second, fields)
    ten_steps(a, b, coef)
    size = 64

    def back(block):
        for f in range(fields):
            here = rows_at(size * block, size)
            total = own[f, here, :] + a[f, rows_at(PAD + ROWS + size * block, size), :]
            grad[f, here, :] = turn(total, -offset(f, fields, width))

    each(height // size, back)


def tables(obs, holder, cell, out, slots):
    profiles = holder.shape[1]
    level_here = lax.axis_index("obs")
    groups = obs.shape[0] // 16
    width = obs.shape[1]
    acc = jnp.zeros((48, profiles), F32)
    row16 = subs((16, width))
    for z in range(groups):
        parts = ([], [], [])
        hots = []
        for c in range(4):
            at = 16 * z + c
            index = obs[pl.ds(at, 1), :].astype(I32)
            w, y, q = (obs[pl.ds(at + 4 * k, 1), :] for k in (1, 2, 3))
            prof = index & 511
            level = (index >> 9) & 7
            field = index >> 12
            low = jnp.where(level == level_here, q, 0.0)
            high = jnp.where(level == level_here - 1, q, 0.0)
            v = 1.0 - w
            lw, hv = low * w, high * v
            rows = (lw * w + hv * v, lw * v, hv * w, (lw + hv) * y)
            value = jnp.where(
                row16 < 8,
                jnp.where(row16 < 4, rows[0], rows[1]),
                jnp.where(row16 < 12, rows[2], rows[3]),
            )
            value = jnp.where((row16 & 3) == field, value, 0.0)
            for part, x in zip(parts, split3(value)):
                part.append(x)
            hots.append(one_hot(subs((profiles, width)) == prof))
        left = jnp.concatenate([jnp.concatenate(p, axis=1) for p in parts], axis=0)
        acc = acc + dot_nt(left, jnp.concatenate(hots, axis=1))
    table = acc[0:16] + acc[16:32] + acc[32:48]
    held = subs((out.shape[0], profiles)) == holder[...]
    held16 = one_hot(held)
    before = one_hot(subs((profiles, profiles)) < lanes((profiles, profiles)))
    slot = jnp.sum(jnp.where(held, dot_nn(held16, before), 0.0), axis=0, keepdims=True)
    slots[...] = slot
    place = slot.astype(I32)
    cells = cell[...].astype(F32)
    mine = [subs((8, profiles)) * 2 + k == place for k in range(2)]
    for k in range(2):
        value = jnp.concatenate(
            [jnp.where(mine[k], table[r : r + 1], 0.0) for r in range(16)], axis=0
        )
        total = sum(dot_nt(held16, part) for part in split3(value))
        out[:, 0, pl.ds(128 * k, 128)] = total
    value = jnp.concatenate(
        [jnp.where(mine[k], cells, 0.0) for k in range(2)]
        + [jnp.zeros((112, profiles), F32)],
        axis=0,
    )
    out[:, 0, pl.ds(256, 128)] = sum(dot_nt(held16, part) for part in split3(value)[:2])


def gather(inc, sent, found, tab, hold):
    fields = inc.shape[0]
    tab[pl.ds(0, 128), :] = jnp.concatenate([sent[:, 0, pl.ds(0, 128)], sent[:, 0, pl.ds(128, 128)]], axis=0).T
    cells = sent[:, 0, pl.ds(256, 128)]
    cells = jnp.concatenate([cells, cells], axis=0).T
    cells = jnp.where(lanes((8, 128)) < 64, cells[0:8], cells[8:16])
    tab[pl.ds(128, 8), :] = cells
    cells = cells.astype(I32)
    left = jnp.concatenate(
        [jnp.concatenate(split3(inc[f]), axis=1) for f in range(fields)], axis=0
    )
    for pair in range(4):
        hots, lats = [], []
        for s in (2 * pair, 2 * pair + 1):
            row = cells[s : s + 1]
            hots.append(one_hot(subs((128, 128)) == (row & 127)))
            lats.append(subs((128, 128)) == (row >> 7))
        hot = jnp.concatenate(hots, axis=1)
        hit = dot_nn(left, jnp.concatenate([hot, hot, hot], axis=0))
        for f in range(fields):
            for i in range(2):
                part = hit[128 * f : 128 * (f + 1), 128 * i : 128 * (i + 1)]
                hold[pl.ds(8 * f + 2 * pair + i, 1), :] = jnp.sum(
                    jnp.where(lats[i], part, 0.0), axis=0, keepdims=True
                )
    rows = hold[...]
    for z in range(found.shape[0] // rows.shape[0]):
        found[pl.ds(z * rows.shape[0], rows.shape[0]), :] = rows


def scatter(levels, tab, pulled, east, west, columns):
    fields = pulled.shape[0]
    rows = 8 * fields
    here = lax.axis_index("obs")
    top = levels.shape[0] // rows - 1

    def level(k):
        return levels[pl.ds(pl.multiple_of(jnp.clip(k, 0, top) * rows, rows), rows), :]

    own, above, below = level(here), level(here + 1), level(here - 1)
    d, o, u, b = (tab[pl.ds(rows * k, rows), :] for k in range(4))
    amount = d * own + o * above + u * below - b
    cells = tab[pl.ds(4 * rows, 8), :].astype(I32)
    lat = [subs((128, 128)) == (cells[s : s + 1] >> 7) for s in range(8)]
    hot = jnp.concatenate(
        [one_hot(subs((128, 128)) == (cells[s : s + 1] & 127)) for s in range(8)], axis=1
    )
    planes = []
    for f in range(fields):
        total = jnp.zeros((128, 128), F32)
        for part in split3(amount[8 * f : 8 * f + 8]):
            wide = part.astype(F32)
            left = jnp.concatenate(
                [jnp.where(lat[s], wide[s : s + 1], 0.0).astype(BF16) for s in range(8)], axis=1
            )
            total = total + dot_nt(left, hot)
        planes.append(turn(total, offset(f, fields, 128)))
        pulled[f] = planes[f]
    pack_edges(planes, (), east, west)
    for half in range(2):
        turned_block = levels[pl.ds(128 * half, 128), :].T
        for k in range(2):
            columns[:, 2 * k + half, :] = turned_block[64 * k : 64 * (k + 1)]


def depart(columns, holder, slots, prof, field, level, weight, innov, prec, out):
    profiles = holder.shape[1]
    left = jnp.concatenate(
        [
            jnp.concatenate([columns[:, half, :], columns[:, 2 + half, :]], axis=0).T
            for half in range(2)
        ],
        axis=0,
    )
    place = slots[...].astype(I32)
    row = subs((128, profiles))
    held = one_hot(((row & 63) == holder[...]) & ((row >> 6) == (place & 1)))
    spread = dot_nn(
        jnp.concatenate(split3(left), axis=1), jnp.concatenate([held, held, held], axis=0)
    )
    mine = subs((8, profiles)) == (place >> 1)
    values = jnp.concatenate(
        [
            jnp.sum(jnp.where(mine, spread[8 * r : 8 * r + 8], 0.0), axis=0, keepdims=True)
            for r in range(32)
        ],
        axis=0,
    )
    hot = jnp.concatenate(
        [one_hot(subs((profiles, 128)) == prof[pl.ds(c, 1), :]) for c in range(4)], axis=1
    )
    seen = sum(dot_nn(part, hot) for part in split3(values))
    row = subs((32, 128))
    for c in range(4):
        at = pl.ds(c, 1)
        code = level[at, :] * 4 + field[at, :]
        part = seen[:, 128 * c : 128 * (c + 1)]
        low = jnp.sum(jnp.where(row == code, part, 0.0), axis=0, keepdims=True)
        high = jnp.sum(jnp.where(row == code + 4, part, 0.0), axis=0, keepdims=True)
        w = weight[at, :]
        out[at, :] = prec[at, :] * (w * low + (1.0 - w) * high - innov[at, :])


def ring(axis, by):
    count = lax.axis_size(axis)
    return [(i, (i + by) % count) for i in range(count)]


def pair(forward, back, axis):
    return (
        lax.ppermute(forward, axis, ring(axis, 1)),
        lax.ppermute(back, axis, ring(axis, -1)),
    )


def swap(first, second, axis):
    count = lax.axis_size(axis)
    low = [(i, i ^ 1) for i in range(count)]
    high = [(i, (i + 1 ^ 1) - 1) for i in range(1, count - 1)]
    first = lax.ppermute(first, axis, low)
    second = lax.ppermute(second, axis, high)
    return first, second


def exchange(x, axes):
    return lax.all_to_all(x, axes, 0, 0, tiled=True)


def assimilate(
    control,
    diffusivity,
    prof_tile,
    prof_cell,
    obs_prof,
    obs_field,
    obs_level,
    obs_weight,
    innovation,
    obs_precision,
):
    fields, _, ny, nx = control.shape
    tile = (ny, nx)
    profiles = prof_tile.shape[0]
    holders = lax.axis_size("gx") * lax.axis_size("gy")
    levels = lax.axis_size("obs")
    ext = ny + 2 * ROWS
    ctl = control.reshape(fields, ny, nx)
    rate = diffusivity.reshape(2, ny, nx)
    holder = prof_tile.reshape(1, profiles)
    cell = prof_cell.reshape(1, profiles)
    obs = [
        x.reshape(4, 128)
        for x in (obs_prof, obs_field, obs_level, obs_weight, innovation, obs_precision)
    ]
    planes = pltpu.VMEM((fields + 1, ext + 2 * PAD, nx), F32)
    coefs = (ext // 8, 5 * (fields + 1), 8, nx)

    given = [
        pltpu.with_memory_space_constraint(x, pltpu.HBM)
        for x in (ctl, rate, holder, cell, *obs)
    ]
    east, west, rows, own, rate, holder, cell, *obs = call(
        pack_inputs,
        [tile, tile, (levels * 16, 128), ctl.shape]
        + [jax.ShapeDtypeStruct(x.shape, x.dtype) for x in given[1:]],
        given,
        [pltpu.VMEM(ctl.shape, F32), pltpu.SemaphoreType.DMA((len(given),))],
        hbm=True,
    )
    left, right = pair(east, west, "gx")
    rows = exchange(rows, "obs")
    side = (fields + 3, ROWS, nx)
    strip, first, second = call(edges_first, [tile, side, side], [own, rate, left, right])
    first, second = swap(first, second, "gy")
    table, slots = call(
        tables, [(holders, 1, 384), (1, profiles)], [rows, holder, cell], flops=400_000_000
    )
    table = exchange(table, ("gx", "gy"))
    inc, coef = call(
        diffuse_control,
        [(fields, ny, nx), coefs],
        [own, rate, strip, first, second],
        [
            planes,
            planes,
            pltpu.VMEM((2, ext + 2 * PAD, nx), F32),
            planes,
        ],
        flops=40_000_000,
    )
    found, tab = call(
        gather,
        [(levels * fields * 8, 128), (136, 128)],
        [inc, table],
        [pltpu.VMEM((fields * 8, 128), F32)],
        flops=400_000_000,
    )
    found = exchange(found, "obs")
    pulled, east, west, columns = call(
        scatter,
        [(fields, ny, nx), tile, tile, (holders, 4, 128)],
        [found, tab],
        flops=400_000_000,
    )
    left, right = pair(east, west, "gx")
    columns = exchange(columns, ("gx", "gy"))
    side = (fields + 1, ROWS, nx)
    strip, first, second = call(edges_second, [tile, side, side], [pulled, left, right])
    first, second = swap(first, second, "gy")
    (gradient,) = call(
        diffuse_pulled,
        [(fields, ny, nx)],
        [pulled, strip, first, second, coef, own],
        [planes, planes],
        flops=40_000_000,
    )
    (departures,) = call(depart, [(4, 128)], [columns, holder, slots, *obs], flops=400_000_000)
    return gradient.reshape(control.shape), departures.reshape(obs_prof.shape)


def solution(mesh):
    in_specs = (
        P(None, "obs", "gy", "gx"),
        P(None, "obs", "gy", "gx"),
        P(("gx", "gy"), None),
        P(("gx", "gy")),
        P(("gx", "gy", "obs")),
        P(("gx", "gy", "obs")),
        P(("gx", "gy", "obs")),
        P(("gx", "gy", "obs")),
        P(("gx", "gy", "obs")),
        P(("gx", "gy", "obs")),
    )
    out_specs = (P(None, "obs", "gy", "gx"), P(("gx", "gy", "obs")))
    return jax.shard_map(
        assimilate, mesh=mesh, in_specs=in_specs, out_specs=out_specs, check_vma=False
    )
```

```python
import jax
import jax.numpy as jnp
from jax import lax
from jax.experimental import pallas as pl
from jax.experimental.pallas import tpu as pltpu
from jax.sharding import PartitionSpec as P


STEPS = 10
HALO = STEPS
ROWS = 16
EAST_AT, NORTH_AT = HALO, 74
PAD = 8
F32, BF16, I32 = jnp.float32, jnp.bfloat16, jnp.int32


def lanes(shape):
    return lax.broadcasted_iota(I32, shape, len(shape) - 1)


def subs(shape):
    return lax.broadcasted_iota(I32, shape, len(shape) - 2)


def split3(x):
    hi = x.astype(BF16)
    rest = x - hi.astype(F32)
    mid = rest.astype(BF16)
    low = (rest - mid.astype(F32)).astype(BF16)
    return hi, mid, low


def one_hot(flags):
    return jnp.where(flags, 1.0, 0.0).astype(BF16)


def dot_nn(a, b):
    return lax.dot_general(a, b, (((1,), (0,)), ((), ())), preferred_element_type=F32)


def dot_nt(a, b):
    return lax.dot_general(a, b, (((1,), (1,)), ((), ())), preferred_element_type=F32)


def call(body, outs, args, scratch=(), flops=1_000_000, hbm=False):
    vmem = pl.BlockSpec(memory_space=pltpu.VMEM)
    given = pl.BlockSpec(memory_space=pltpu.HBM) if hbm else vmem
    outs = [o if isinstance(o, jax.ShapeDtypeStruct) else jax.ShapeDtypeStruct(o, F32) for o in outs]
    return pl.pallas_call(
        body,
        out_shape=outs,
        in_specs=[given] * len(args),
        out_specs=[vmem] * len(outs),
        scratch_shapes=list(scratch),
        cost_estimate=pl.CostEstimate(
            flops=flops,
            bytes_accessed=sum(4 * x.size for x in (*args, *outs)),
            transcendentals=0,
        ),
        compiler_params=pltpu.CompilerParams(vmem_limit_bytes=16 << 20),
    )(*args)


def mask_north(rate_ref):
    last = rate_ref.shape[1] - 8
    rows = rate_ref[1, pl.ds(last, 8), :]
    top = lax.axis_index("gy") == lax.axis_size("gy") - 1
    rate_ref[1, pl.ds(last, 8), :] = jnp.where(top & (subs(rows.shape) == 7), 0.0, rows)


def offset(f, planes, width):
    return f * (width // planes)


def turn(x, by):
    by %= x.shape[-1]
    return pltpu.roll(x, by, x.ndim - 1) if by else x


def within(shape, low):
    width = shape[-1]
    return ((lanes(shape) - low % width + width) & (width - 1)) < HALO


def pack_edges(turned, rates, east_ref, west_ref):
    shape = turned[0].shape
    width = shape[-1]
    east = west = jnp.zeros(shape, F32)
    for f, x in enumerate(turned):
        low = offset(f, len(turned), width)
        east = jnp.where(within(shape, low - HALO), x, east)
        west = jnp.where(within(shape, low), x, west)
    for at, x in rates:
        east = jnp.where(within(shape, at), turn(x, at + HALO - width), east)
        west = jnp.where(within(shape, at + 32), turn(x, at + 32), west)
    east_ref[...] = east
    west_ref[...] = west


def pack_inputs(*refs):
    sources, (east, west, obs, turned), kept, (ctl, sems) = refs[:10], refs[10:14], refs[14:23], refs[23:]
    copies = [
        pltpu.make_async_copy(source, target, sems.at[i])
        for i, (source, target) in enumerate(zip(sources, (ctl, *kept)))
    ]
    for copy in copies:
        copy.start()
    for copy in copies:
        copy.wait()
    rate, _, _, prof, field, level, weight, innov, prec = kept
    mask_north(rate)
    fields = ctl.shape[0]
    planes = [turn(ctl[f], offset(f, fields, ctl.shape[2])) for f in range(fields)]
    for f in range(fields):
        turned[f] = planes[f]
    pack_edges(planes, ((EAST_AT, rate[0]), (NORTH_AT, rate[1])), east, west)
    index = ((field[...] * 8 + level[...]) * 512 + prof[...]).astype(F32)
    rows = jnp.concatenate([index, weight[...], innov[...], prec[...]], axis=0)
    for z in range(obs.shape[0] // rows.shape[0]):
        obs[pl.ds(z * rows.shape[0], rows.shape[0]), :] = rows


def odd():
    return lax.rem(lax.axis_index("gy"), 2)


def pick(first, second):
    return pl.multiple_of(jnp.where(odd() == 0, first, second), 8)


def meet(refs, strip, first, second):
    last = strip.shape[0] - ROWS
    for target, at in ((first, pick(last, 0)), (second, pick(0, last))):
        for a, ref in enumerate(refs + [strip]):
            target[a] = ref[pl.ds(at, ROWS), :]


def edges_first(own, rate, left, right, strip, first, second):
    strip[...] = left[...] + right[...]
    refs = [own.at[f] for f in range(own.shape[0])] + [rate.at[0], rate.at[1]]
    meet(refs, strip, first, second)


def edges_second(pulled, left, right, strip, first, second):
    strip[...] = left[...] + right[...]
    meet([pulled.at[f] for f in range(pulled.shape[0])], strip, first, second)


def blocks(own, first, second):
    low, high = PAD, PAD + ROWS + own.shape[0]
    return ((pick(high, low), first), (PAD + ROWS, own), (pick(low, high), second))


def one_step(source, target, coef):
    fields = source.shape[0] - 1
    width = source.shape[2]
    for tile in range(coef.shape[0]):
        row = PAD + 8 * tile
        here, up, down = pl.ds(row, 8), pl.ds(row + 1, 8), pl.ds(row - 1, 8)
        lane = lanes((8, width))

        def new(p, v, east, west):
            c = [coef[tile, 5 * p + i] for i in range(5)]
            total = c[0] * v + c[1] * east + c[2] * west
            target[p, here, :] = total + c[3] * source[p, up, :] + c[4] * source[p, down, :]

        strip = source[fields, here, :]
        strip_east = next_east = turn(strip, -1)
        strip_west = next_west = turn(strip, 1)
        for f in range(fields):
            v = source[f, here, :]
            start = lane == offset(f, fields, width)
            stop = lane == (offset(f, fields, width) - 1) % width
            east, west = turn(v, -1), turn(v, 1)
            next_east = jnp.where(stop, east, next_east)
            next_west = jnp.where(start, west, next_west)
            new(f, v, jnp.where(stop, strip_east, east), jnp.where(start, strip_west, west))
        new(fields, strip, next_east, next_west)


def ten_steps(a, b, coef):
    def body(_):
        one_step(a, b, coef)
        one_step(b, a, coef)

    each(STEPS // 2, body)


def each(count, body):
    def step(i, carry):
        body(i)
        return carry

    lax.fori_loop(0, count, step, 0)


def rows_at(start, size):
    return pl.ds(pl.multiple_of(start, 8), size)


def clear_ends(a):
    clear = jnp.zeros((PAD, a.shape[2]), F32)
    for plane in range(a.shape[0]):
        a[plane, pl.ds(0, PAD), :] = clear
        a[plane, pl.ds(a.shape[1] - PAD, PAD), :] = clear


def load_field(a, b, own, strip, first, second, packed):
    fields = own.shape[0]
    for f in range(fields):
        for row, block in blocks(own[f], first[f], second[f]):
            a[f, pl.ds(row, block.shape[0]), :] = block
    for row, block in blocks(strip[...], first[packed], second[packed]):
        a[fields, pl.ds(row, block.shape[0]), :] = block
    clear_ends(a)
    clear_ends(b)


def rate_strip(packed, at, fields):
    shape = packed.shape
    width = shape[-1]
    east = turn(packed, -at - 32)
    west = turn(packed, width - HALO - at)
    g = jnp.where(within(shape, 0), east, jnp.where(within(shape, -HALO), west, 0.0))
    by = width // fields
    while by < width:
        g = g + turn(g, by)
        by *= 2
    return g


def diffuse_control(own, rate, strip, first, second, inc, coef, a, b, wide, north):
    fields, height, width = own.shape
    load_field(a, b, own, strip, first, second, fields + 2)
    for k in range(2):
        for row, block in blocks(rate[k], first[fields + k], second[fields + k]):
            wide[k, pl.ds(row, block.shape[0]), :] = block
    north[:, pl.ds(0, PAD), :] = jnp.zeros((fields + 1, PAD, width), F32)
    size = 80

    def turned(block):
        here = rows_at(PAD + size * block, size)
        n = wide[1, here, :]
        for f in range(fields):
            north[f, here, :] = turn(n, offset(f, fields, width))
        north[fields, here, :] = rate_strip(a[fields, here, :], NORTH_AT, fields)
        for k in range(size // 8):
            tile = size // 8 * block + k
            e = wide[0, rows_at(PAD + 8 * tile, 8), :]
            beyond = rate_strip(a[fields, rows_at(PAD + 8 * tile, 8), :], EAST_AT, fields)
            before = strip_before = turn(beyond, 1)
            lane = lanes((8, width))
            planes = []
            for f in range(fields):
                low = offset(f, fields, width)
                start = lane == low
                moved = turn(e, low + 1)
                strip_before = jnp.where(start, moved, strip_before)
                planes.append((turn(e, low), jnp.where(start, before, moved)))
            planes.append((beyond, strip_before))
            for p, (east, west) in enumerate(planes):
                both = north[p, rows_at(8 * tile, 16), :]
                n, s = both[8:], both[7:15]
                for i, value in enumerate((1.0 - east - west - n - s, east, west, n, s)):
                    coef[tile, 5 * p + i] = value

    each(coef.shape[0] * 8 // size, turned)
    ten_steps(a, b, coef)
    size = 128

    def back(block):
        for f in range(fields):
            value = a[f, rows_at(PAD + ROWS + size * block, size), :]
            inc[f, rows_at(size * block, size), :] = turn(value, -offset(f, fields, width))

    each(height // size, back)


def diffuse_pulled(pulled, strip, first, second, coef, own, grad, a, b):
    fields, height, width = pulled.shape
    load_field(a, b, pulled, strip, first, second, fields)
    ten_steps(a, b, coef)
    size = 128

    def back(block):
        for f in range(fields):
            here = rows_at(size * block, size)
            total = own[f, here, :] + a[f, rows_at(PAD + ROWS + size * block, size), :]
            grad[f, here, :] = turn(total, -offset(f, fields, width))

    each(height // size, back)


def tables(obs, holder, cell, out, slots):
    profiles = holder.shape[1]
    level_here = lax.axis_index("obs")
    groups = obs.shape[0] // 16
    width = obs.shape[1]
    acc = jnp.zeros((48, profiles), F32)
    row16 = subs((16, width))
    for z in range(groups):
        parts = ([], [], [])
        hots = []
        for c in range(4):
            at = 16 * z + c
            index = obs[pl.ds(at, 1), :].astype(I32)
            w, y, q = (obs[pl.ds(at + 4 * k, 1), :] for k in (1, 2, 3))
            prof = index & 511
            level = (index >> 9) & 7
            field = index >> 12
            low = jnp.where(level == level_here, q, 0.0)
            high = jnp.where(level == level_here - 1, q, 0.0)
            v = 1.0 - w
            lw, hv = low * w, high * v
            rows = (lw * w + hv * v, lw * v, hv * w, (lw + hv) * y)
            value = jnp.where(
                row16 < 8,
                jnp.where(row16 < 4, rows[0], rows[1]),
                jnp.where(row16 < 12, rows[2], rows[3]),
            )
            value = jnp.where((row16 & 3) == field, value, 0.0)
            for part, x in zip(parts, split3(value)):
                part.append(x)
            hots.append(one_hot(subs((profiles, width)) == prof))
        left = jnp.concatenate([jnp.concatenate(p, axis=1) for p in parts], axis=0)
        acc = acc + dot_nt(left, jnp.concatenate(hots, axis=1))
    table = acc[0:16] + acc[16:32] + acc[32:48]
    held = subs((out.shape[0], profiles)) == holder[...]
    held16 = one_hot(held)
    before = one_hot(subs((profiles, profiles)) < lanes((profiles, profiles)))
    slot = jnp.sum(jnp.where(held, dot_nn(held16, before), 0.0), axis=0, keepdims=True)
    slots[...] = slot
    place = slot.astype(I32)
    cells = cell[...].astype(F32)
    mine = [subs((8, profiles)) * 2 + k == place for k in range(2)]
    for k in range(2):
        value = jnp.concatenate(
            [jnp.where(mine[k], table[r : r + 1], 0.0) for r in range(16)], axis=0
        )
        total = sum(dot_nt(held16, part) for part in split3(value))
        out[:, 0, pl.ds(128 * k, 128)] = total
    value = jnp.concatenate(
        [jnp.where(mine[k], cells, 0.0) for k in range(2)]
        + [jnp.zeros((112, profiles), F32)],
        axis=0,
    )
    out[:, 0, pl.ds(256, 128)] = sum(dot_nt(held16, part) for part in split3(value)[:2])


def gather(inc, sent, found, tab, hold):
    fields = inc.shape[0]
    tab[pl.ds(0, 128), :] = jnp.concatenate([sent[:, 0, pl.ds(0, 128)], sent[:, 0, pl.ds(128, 128)]], axis=0).T
    cells = sent[:, 0, pl.ds(256, 128)]
    cells = jnp.concatenate([cells, cells], axis=0).T
    cells = jnp.where(lanes((8, 128)) < 64, cells[0:8], cells[8:16])
    tab[pl.ds(128, 8), :] = cells
    cells = cells.astype(I32)
    left = jnp.concatenate(
        [jnp.concatenate(split3(inc[f]), axis=1) for f in range(fields)], axis=0
    )
    for pair in range(4):
        hots, lats = [], []
        for s in (2 * pair, 2 * pair + 1):
            row = cells[s : s + 1]
            hots.append(one_hot(subs((128, 128)) == (row & 127)))
            lats.append(subs((128, 128)) == (row >> 7))
        hot = jnp.concatenate(hots, axis=1)
        hit = dot_nn(left, jnp.concatenate([hot, hot, hot], axis=0))
        for f in range(fields):
            for i in range(2):
                part = hit[128 * f : 128 * (f + 1), 128 * i : 128 * (i + 1)]
                hold[pl.ds(8 * f + 2 * pair + i, 1), :] = jnp.sum(
                    jnp.where(lats[i], part, 0.0), axis=0, keepdims=True
                )
    rows = hold[...]
    for z in range(found.shape[0] // rows.shape[0]):
        found[pl.ds(z * rows.shape[0], rows.shape[0]), :] = rows


def scatter(levels, tab, pulled, east, west, columns):
    fields = pulled.shape[0]
    rows = 8 * fields
    here = lax.axis_index("obs")
    top = levels.shape[0] // rows - 1

    def level(k):
        return levels[pl.ds(pl.multiple_of(jnp.clip(k, 0, top) * rows, rows), rows), :]

    own, above, below = level(here), level(here + 1), level(here - 1)
    d, o, u, b = (tab[pl.ds(rows * k, rows), :] for k in range(4))
    amount = d * own + o * above + u * below - b
    cells = tab[pl.ds(4 * rows, 8), :].astype(I32)
    lat = [subs((128, 128)) == (cells[s : s + 1] >> 7) for s in range(8)]
    hot = jnp.concatenate(
        [one_hot(subs((128, 128)) == (cells[s : s + 1] & 127)) for s in range(8)], axis=1
    )
    planes = []
    for f in range(fields):
        total = jnp.zeros((128, 128), F32)
        for part in split3(amount[8 * f : 8 * f + 8]):
            wide = part.astype(F32)
            left = jnp.concatenate(
                [jnp.where(lat[s], wide[s : s + 1], 0.0).astype(BF16) for s in range(8)], axis=1
            )
            total = total + dot_nt(left, hot)
        planes.append(turn(total, offset(f, fields, 128)))
        pulled[f] = planes[f]
    pack_edges(planes, (), east, west)
    for half in range(2):
        turned_block = levels[pl.ds(128 * half, 128), :].T
        for k in range(2):
            columns[:, 2 * k + half, :] = turned_block[64 * k : 64 * (k + 1)]


def depart(columns, holder, slots, prof, field, level, weight, innov, prec, out):
    profiles = holder.shape[1]
    left = jnp.concatenate(
        [
            jnp.concatenate([columns[:, half, :], columns[:, 2 + half, :]], axis=0).T
            for half in range(2)
        ],
        axis=0,
    )
    place = slots[...].astype(I32)
    row = subs((128, profiles))
    held = one_hot(((row & 63) == holder[...]) & ((row >> 6) == (place & 1)))
    spread = dot_nn(
        jnp.concatenate(split3(left), axis=1), jnp.concatenate([held, held, held], axis=0)
    )
    mine = subs((8, profiles)) == (place >> 1)
    values = jnp.concatenate(
        [
            jnp.sum(jnp.where(mine, spread[8 * r : 8 * r + 8], 0.0), axis=0, keepdims=True)
            for r in range(32)
        ],
        axis=0,
    )
    hot = jnp.concatenate(
        [one_hot(subs((profiles, 128)) == prof[pl.ds(c, 1), :]) for c in range(4)], axis=1
    )
    seen = dot_nn(jnp.concatenate(split3(values), axis=0), hot)
    seen = seen[0:32] + seen[32:64] + seen[64:96]
    row = subs((32, 128))
    for c in range(4):
        at = pl.ds(c, 1)
        code = level[at, :] * 4 + field[at, :]
        part = seen[:, 128 * c : 128 * (c + 1)]
        low = jnp.sum(jnp.where(row == code, part, 0.0), axis=0, keepdims=True)
        high = jnp.sum(jnp.where(row == code + 4, part, 0.0), axis=0, keepdims=True)
        w = weight[at, :]
        out[at, :] = prec[at, :] * (w * low + (1.0 - w) * high - innov[at, :])


def ring(axis, by):
    count = lax.axis_size(axis)
    return [(i, (i + by) % count) for i in range(count)]


def pair(forward, back, axis):
    return (
        lax.ppermute(forward, axis, ring(axis, 1)),
        lax.ppermute(back, axis, ring(axis, -1)),
    )


def swap(first, second, axis):
    count = lax.axis_size(axis)
    low = [(i, i ^ 1) for i in range(count)]
    high = [(i, (i + 1 ^ 1) - 1) for i in range(1, count - 1)]
    return lax.ppermute(first, axis, low), lax.ppermute(second, axis, high)


def exchange(x, axes):
    return lax.all_to_all(x, axes, 0, 0, tiled=True)


def assimilate(
    control,
    diffusivity,
    prof_tile,
    prof_cell,
    obs_prof,
    obs_field,
    obs_level,
    obs_weight,
    innovation,
    obs_precision,
):
    fields, _, ny, nx = control.shape
    tile = (ny, nx)
    profiles = prof_tile.shape[0]
    holders = lax.axis_size("gx") * lax.axis_size("gy")
    levels = lax.axis_size("obs")
    ext = ny + 2 * ROWS
    ctl = control.reshape(fields, ny, nx)
    rate = diffusivity.reshape(2, ny, nx)
    holder = prof_tile.reshape(1, profiles)
    cell = prof_cell.reshape(1, profiles)
    obs = [
        x.reshape(4, 128)
        for x in (obs_prof, obs_field, obs_level, obs_weight, innovation, obs_precision)
    ]
    planes = pltpu.VMEM((fields + 1, ext + 2 * PAD, nx), F32)
    coefs = (ext // 8, 5 * (fields + 1), 8, nx)

    given = [
        pltpu.with_memory_space_constraint(x, pltpu.HBM)
        for x in (ctl, rate, holder, cell, *obs)
    ]
    east, west, rows, own, rate, holder, cell, *obs = call(
        pack_inputs,
        [tile, tile, (levels * 16, 128), ctl.shape]
        + [jax.ShapeDtypeStruct(x.shape, x.dtype) for x in given[1:]],
        given,
        [pltpu.VMEM(ctl.shape, F32), pltpu.SemaphoreType.DMA((len(given),))],
        hbm=True,
    )
    left, right = pair(east, west, "gx")
    rows = exchange(rows, "obs")
    side = (fields + 3, ROWS, nx)
    strip, first, second = call(edges_first, [tile, side, side], [own, rate, left, right])
    first, second = swap(first, second, "gy")
    table, slots = call(
        tables, [(holders, 1, 384), (1, profiles)], [rows, holder, cell], flops=400_000_000
    )
    table = exchange(table, ("gx", "gy"))
    inc, coef = call(
        diffuse_control,
        [(fields, ny, nx), coefs],
        [own, rate, strip, first, second],
        [
            planes,
            planes,
            pltpu.VMEM((2, ext + 2 * PAD, nx), F32),
            planes,
        ],
        flops=40_000_000,
    )
    found, tab = call(
        gather,
        [(levels * fields * 8, 128), (136, 128)],
        [inc, table],
        [pltpu.VMEM((fields * 8, 128), F32)],
        flops=400_000_000,
    )
    found = exchange(found, "obs")
    pulled, east, west, columns = call(
        scatter,
        [(fields, ny, nx), tile, tile, (holders, 4, 128)],
        [found, tab],
        flops=400_000_000,
    )
    left, right = pair(east, west, "gx")
    columns = exchange(columns, ("gx", "gy"))
    side = (fields + 1, ROWS, nx)
    strip, first, second = call(edges_second, [tile, side, side], [pulled, left, right])
    first, second = swap(first, second, "gy")
    (gradient,) = call(
        diffuse_pulled,
        [(fields, ny, nx)],
        [pulled, strip, first, second, coef, own],
        [planes, planes],
        flops=40_000_000,
    )
    (departures,) = call(depart, [(4, 128)], [columns, holder, slots, *obs], flops=400_000_000)
    return gradient.reshape(control.shape), departures.reshape(obs_prof.shape)


def solution(mesh):
    in_specs = (
        P(None, "obs", "gy", "gx"),
        P(None, "obs", "gy", "gx"),
        P(("gx", "gy"), None),
        P(("gx", "gy")),
        P(("gx", "gy", "obs")),
        P(("gx", "gy", "obs")),
        P(("gx", "gy", "obs")),
        P(("gx", "gy", "obs")),
        P(("gx", "gy", "obs")),
        P(("gx", "gy", "obs")),
    )
    out_specs = (P(None, "obs", "gy", "gx"), P(("gx", "gy", "obs")))
    return jax.shard_map(
        assimilate, mesh=mesh, in_specs=in_specs, out_specs=out_specs, check_vma=False
    )
```
